32 devices in a mesh: shard: 4 (over y, core), ctx: 2 (over x), tp: 4 (over z).
Axes of the slice: x: 2, y: 2, z: 4, core: 2. Of those that a mesh axis runs over, the one named last changes fastest.
Arguments:
- block_in: bfloat16 [4, 256, 768], P('shard', 'ctx'), may hold values from -6 to 6
- segment_ids: int32 [4, 256], P('shard', 'ctx'), may hold values from 0 to 3, never falling along the last dimension, each value on 1 to 128 neighbouring positions
- out_cotangent: bfloat16 [4, 256, 768], P('shard', 'ctx'), may hold values from -6 to 6
- attn_gain: bfloat16 [768], P('shard'), may hold values from 0.5 to 1.5
- attn_shift: bfloat16 [768], P('shard'), may hold values from -2.5 to 2.5
- qkv_weight: bfloat16 [768, 3, 768], P('shard', None, 'tp'), may hold values from -4 to 4
- qv_bias: bfloat16 [2, 12, 64], P(None, 'tp', 'shard'), may hold values from -2.5 to 2.5
- proj_weight: bfloat16 [768, 768], P('tp', 'shard'), may hold values from -1.75 to 1.75
- proj_bias: bfloat16 [768], P('shard'), may hold values from -3 to 3
- mlp_gain: bfloat16 [768], P('shard'), may hold values from 0.5 to 1.5
- mlp_shift: bfloat16 [768], P('shard'), may hold values from -2.5 to 2.5
- up_weight: bfloat16 [768, 3072], P('shard', 'tp'), may hold values from -0.21875 to 0.21875
- up_bias: bfloat16 [24, 128], P('tp', 'shard'), may hold values from -3 to 3
- down_weight: bfloat16 [3072, 768], P('tp', 'shard'), may hold values from -0.109375 to 0.109375
- down_bias: bfloat16 [768], P('shard'), may hold values from -3 to 3
Outputs:
- block_out: float32 [4, 256, 768], P('shard', 'ctx')
- block_in_grad: float32 [4, 256, 768], P('shard', 'ctx')
- attn_gain_grad: float32 [768], P('shard')
- attn_shift_grad: float32 [768], P('shard')
- qkv_weight_grad: float32 [768, 3, 768], P('shard', None, 'tp')
- qv_bias_grad: float32 [2, 12, 64], P(None, 'tp', 'shard')
- proj_weight_grad: float32 [768, 768], P('tp', 'shard')
- proj_bias_grad: float32 [768], P('shard')
- mlp_gain_grad: float32 [768], P('shard')
- mlp_shift_grad: float32 [768], P('shard')
- up_weight_grad: float32 [768, 3072], P('shard', 'tp')
- up_bias_grad: float32 [24, 128], P('tp', 'shard')
- down_weight_grad: float32 [3072, 768], P('tp', 'shard')
- down_bias_grad: float32 [768], P('shard')
The draws below stay inside these ranges and needn't reach their ends.
Inputs may be any that keep to these rules, and one draw needn't show every extreme that they name: `segment_ids`: along each row the numbers never fall; each document holds 1 to 128 tokens, and one document of each row holds exactly 128.
All inputs are finite; a program needn't handle non-finite values.
Results may differ from the reference program's by a relative error of at most 0.0095.
Values may be sent and summed in bfloat16 or wider, within the bound.
A program may use at most 64 MiB of HBM per device.

```python
import math
import jax
import jax.numpy as jnp
import numpy as np
from jax import lax

D = 768
H = 12
HD = 64
FF = 3072
DOCS = 4
ROWS = 4
L = 256


def draw_qkv_weight(key, part):
    values = jnp.clip(jax.random.normal(key, (D, 3, D), jnp.float32), -5.0, 5.0) * D ** (-0.5)
    return values.astype(jnp.bfloat16)


def levels(rng, dims, cuts, smallest, high):
    def one(dim, shards_of):
        draws = jax.random.uniform(jax.random.fold_in(jax.random.fold_in(rng, 6), dim), (shards_of,), jnp.float32, smallest / len(cuts), high / len(cuts))
        return jnp.repeat(jnp.exp(draws), dims[dim] // shards_of).reshape((-1,) + (1,) * (len(dims) - dim - 1))

    factor_of = one(*cuts[0])
    for cut in cuts[1:]:
        factor_of = factor_of * one(*cut)
    return factor_of


def length_profile(amount, total, reach, skew):
    portions = [(1 << 20) // math.isqrt(standing ** skew) + 1 for standing in range(2, amount + 1)]
    spare, counts = total - reach - (amount - 1), [1] * (amount - 1)
    while spare > 0:
        candidates = [i for i in range(amount - 1) if counts[i] < reach]
        mass, remaining = sum([portions[i] for i in candidates]), spare
        for i in candidates:
            addition = min(reach - counts[i], max(1, remaining * portions[i] // mass), spare)
            counts[i] = counts[i] + addition
            spare = spare - addition
    return np.array([reach] + counts)


def uneven_parts(key, number_of, total, bound, slope):
    if number_of == 2:
        one = jax.random.randint(key, (), max(1, total - bound), min(bound, total - 1) + 1)
        return jnp.stack([one, total - one])
    tallies = jnp.asarray(length_profile(number_of, total, bound, slope), jnp.int32)
    twos = (number_of - 1) // 2
    donor, taker = tallies[1:1 + 2 * twos:2], tallies[2:2 + 2 * twos:2]
    slack = jnp.minimum(donor - 1, bound - taker)
    moved = jax.random.randint(jax.random.fold_in(key, 1), (twos,), 0, 1 << 20) % (slack + 1)
    tallies = tallies.at[1:1 + 2 * twos:2].set(donor - moved).at[2:2 + 2 * twos:2].set(taker + moved)
    return tallies[jax.random.permutation(jax.random.fold_in(key, 2), number_of)]


def normal_values(key, dims, deviation, most, cuts=(), held_as=jnp.bfloat16):
    level = levels(key, dims, cuts, -0.22, 0.18) if cuts else 1.0
    array = jax.random.normal(key, dims, jnp.float32) * deviation * level
    return jnp.minimum(jnp.maximum(array, -most), most).astype(held_as)


def setup_inputs(seed: int = 0) -> dict:
    streams_of = jax.random.split(jax.random.key(seed), 16)
    block_in = normal_values(streams_of[0], (ROWS, L, D), 1.0, 6.0, ((0, 4), (1, 2)))
    segment_ids = jax.vmap(lambda own: jnp.searchsorted(jnp.cumsum(uneven_parts(own, DOCS, L, L // 2, 0)), jnp.arange(L), side="right"))(jax.random.split(streams_of[1], ROWS)).reshape((ROWS, L)).astype(jnp.int32)
    out_cotangent = normal_values(streams_of[2], (ROWS, L, D), 1.0, 6.0, ((0, 4), (1, 2)))
    attn_gain = jnp.clip(1.0 + 0.1 * jax.random.normal(streams_of[3], (D,), jnp.float32), 0.5, 1.5).astype(jnp.bfloat16)
    attn_shift = normal_values(streams_of[4], (D,), 0.3, 2.5, ((0, 4),))
    qkv_weight = draw_qkv_weight(jax.random.fold_in(streams_of[15], 71), 0)
    qv_bias = normal_values(streams_of[6], (2, H, HD), 0.3, 2.5, ((1, 4), (2, 4)))
    proj_weight = normal_values(streams_of[7], (D, D), (D // 64) ** -0.5, 1.75, ((0, 4), (1, 4)))
    proj_bias = normal_values(streams_of[8], (D,), 0.8, 3.0, ((0, 4),))
    mlp_gain = jnp.clip(1.0 + 0.1 * jax.random.normal(streams_of[9], (D,), jnp.float32), 0.5, 1.5).astype(jnp.bfloat16)
    mlp_shift = normal_values(streams_of[10], (D,), 0.3, 2.5, ((0, 4),))
    up_weight = normal_values(streams_of[11], (D, FF), D ** -0.5, 0.21875, ((0, 4), (1, 4)))
    up_bias = normal_values(streams_of[12], (FF // 128, 128), 0.5, 3.0, ((0, 4), (1, 4)))
    down_weight = normal_values(streams_of[13], (FF, D), FF ** -0.5, 0.109375, ((0, 4), (1, 4)))
    down_bias = normal_values(streams_of[14], (D,), 1.0, 3.0, ((0, 4),))
    return {"block_in": block_in, "segment_ids": segment_ids, "out_cotangent": out_cotangent, "attn_gain": attn_gain, "attn_shift": attn_shift, "qkv_weight": qkv_weight, "qv_bias": qv_bias, "proj_weight": proj_weight, "proj_bias": proj_bias, "mlp_gain": mlp_gain, "mlp_shift": mlp_shift, "up_weight": up_weight, "up_bias": up_bias, "down_weight": down_weight, "down_bias": down_bias}


EPSILON = 1e-05
GELU_ROOT = math.sqrt(2.0 / math.pi)
GELU_CUBIC = 0.044715
SCORE_SCALE = 0.125

def normalize(values, gain_vec, offset):
    center = lax.optimization_barrier(jnp.mean(values, axis=-1, keepdims=True))
    shifted = values - center
    spread = lax.optimization_barrier(jnp.mean(shifted * shifted, axis=-1, keepdims=True))
    inverse = lax.rsqrt(spread + EPSILON)
    unit_vals = shifted * inverse
    return (unit_vals, inverse, unit_vals * gain_vec + offset)

def normalize_back(grad_norm, unit_vals, inverse, gain_vec):
    scaled = grad_norm * gain_vec
    mean_first = lax.optimization_barrier(jnp.mean(scaled, axis=-1, keepdims=True))
    second = lax.optimization_barrier(jnp.mean(scaled * unit_vals, axis=-1, keepdims=True))
    return inverse * (scaled - mean_first - unit_vals * second)

def gelu_value(pre_gelu):
    return 0.5 * pre_gelu * (1.0 + jnp.tanh(GELU_ROOT * (pre_gelu + GELU_CUBIC * pre_gelu * pre_gelu * pre_gelu)))

def gelu_slope(pre_gelu):
    tangent = jnp.tanh(GELU_ROOT * (pre_gelu + GELU_CUBIC * pre_gelu * pre_gelu * pre_gelu))
    return 0.5 * (1.0 + tangent) + 0.5 * pre_gelu * (1.0 - tangent * tangent) * GELU_ROOT * (1.0 + 3.0 * GELU_CUBIC * pre_gelu * pre_gelu)

def reference(block_in, segment_ids, out_cotangent, attn_gain, attn_shift, qkv_weight, qv_bias, proj_weight, proj_bias, mlp_gain, mlp_shift, up_weight, up_bias, down_weight, down_bias):
    gain_one = attn_gain.astype(jnp.float32)
    shift_one = attn_shift.astype(jnp.float32)
    gain_two = mlp_gain.astype(jnp.float32)
    shift_two = mlp_shift.astype(jnp.float32)
    proj_offset = proj_bias.astype(jnp.float32)
    down_offset = down_bias.astype(jnp.float32)
    qkv_flat = qkv_weight.reshape(D, 3 * D)
    query_bias = qv_bias[0].reshape(D).astype(jnp.float32)
    value_bias = qv_bias[1].reshape(D).astype(jnp.float32)
    up_offset = up_bias.reshape(FF).astype(jnp.float32)
    positions = jnp.arange(L, dtype=jnp.int32)
    causal = positions[None, :] <= positions[:, None]

    def one_row(carried, row_data):
        row_in, row_segments, row_cot = row_data
        residual_in = row_in.astype(jnp.float32)
        unit_one, inverse_one, normed = normalize(residual_in, gain_one, shift_one)
        normed_one = normed.astype(jnp.bfloat16)
        projected = jnp.dot(normed_one, qkv_flat, preferred_element_type=jnp.float32).reshape(L, 3, D)
        queries = (projected[:, 0] + query_bias).astype(jnp.bfloat16).reshape(L, H, HD)
        keys_low = projected[:, 1].astype(jnp.bfloat16).reshape(L, H, HD)
        values = (projected[:, 2] + value_bias).astype(jnp.bfloat16).reshape(L, H, HD)
        allowed = causal & (row_segments[None, :] == row_segments[:, None])
        scores = jnp.einsum('qhd,khd->hqk', queries.astype(jnp.float32), keys_low.astype(jnp.float32)) * SCORE_SCALE
        scores = jnp.where(allowed[None], scores, -jnp.inf)
        highest = lax.optimization_barrier(jnp.max(scores, axis=-1, keepdims=True))
        log_total = highest + jnp.log(lax.optimization_barrier(jnp.sum(jnp.exp(scores - highest), axis=-1, keepdims=True)))
        probs = jnp.exp(scores - log_total)
        probs_low = probs.astype(jnp.bfloat16)
        mixed = jnp.einsum('hqk,khd->qhd', probs_low.astype(jnp.float32), values.astype(jnp.float32)).astype(jnp.bfloat16)
        mixed_flat = mixed.reshape(L, D)
        residual_mid = residual_in + jnp.dot(mixed_flat, proj_weight, preferred_element_type=jnp.float32) + proj_offset
        unit_two, inverse_two, normed = normalize(residual_mid, gain_two, shift_two)
        normed_two = normed.astype(jnp.bfloat16)
        pre_gelu = jnp.dot(normed_two, up_weight, preferred_element_type=jnp.float32) + up_offset
        hidden = gelu_value(pre_gelu).astype(jnp.bfloat16)
        row_out = residual_mid + jnp.dot(hidden, down_weight, preferred_element_type=jnp.float32) + down_offset
        cot_high = row_cot.astype(jnp.float32)
        down_offset_grad = lax.optimization_barrier(jnp.sum(cot_high, axis=0))
        down_weight_grad = jnp.dot(hidden.T, row_cot, preferred_element_type=jnp.float32)
        pre_grad = jnp.dot(row_cot, down_weight.T, preferred_element_type=jnp.float32) * gelu_slope(pre_gelu)
        up_offset_grad = lax.optimization_barrier(jnp.sum(pre_grad, axis=0)).reshape(FF // 128, 128)
        pre_grad_low = pre_grad.astype(jnp.bfloat16)
        up_weight_grad = jnp.dot(normed_two.T, pre_grad_low, preferred_element_type=jnp.float32)
        norm_two_grad = jnp.dot(pre_grad_low, up_weight.T, preferred_element_type=jnp.float32)
        gain_two_grad = lax.optimization_barrier(jnp.sum(norm_two_grad * unit_two, axis=0))
        shift_two_grad = lax.optimization_barrier(jnp.sum(norm_two_grad, axis=0))
        mid_grad = cot_high + normalize_back(norm_two_grad, unit_two, inverse_two, gain_two)
        proj_offset_grad = lax.optimization_barrier(jnp.sum(mid_grad, axis=0))
        mid_grad_low = mid_grad.astype(jnp.bfloat16)
        proj_weight_grad = jnp.dot(mixed_flat.T, mid_grad_low, preferred_element_type=jnp.float32)
        mixed_grad = jnp.dot(mid_grad_low, proj_weight.T, preferred_element_type=jnp.float32).astype(jnp.bfloat16).reshape(L, H, HD)
        delta = lax.optimization_barrier(jnp.sum(mixed_grad.astype(jnp.float32) * mixed.astype(jnp.float32), axis=-1))
        value_grad = jnp.einsum('hqk,qhd->khd', probs_low.astype(jnp.float32), mixed_grad.astype(jnp.float32))
        weight_grad = jnp.einsum('qhd,khd->hqk', mixed_grad.astype(jnp.float32), values.astype(jnp.float32))
        score_grad = (probs * (weight_grad - delta.T[:, :, None])).astype(jnp.bfloat16)
        query_grad = jnp.einsum('hqk,khd->qhd', score_grad.astype(jnp.float32), keys_low.astype(jnp.float32)) * SCORE_SCALE
        key_grad = jnp.einsum('hqk,qhd->khd', score_grad.astype(jnp.float32), queries.astype(jnp.float32)) * SCORE_SCALE
        qv_grad = jnp.stack([lax.optimization_barrier(jnp.sum(query_grad, axis=0)), lax.optimization_barrier(jnp.sum(value_grad, axis=0))])
        qkv_grad = jnp.stack([query_grad.reshape(L, D), key_grad.reshape(L, D), value_grad.reshape(L, D)], axis=1).astype(jnp.bfloat16).reshape(L, 3 * D)
        qkv_weight_grad = jnp.dot(normed_one.T, qkv_grad, preferred_element_type=jnp.float32).reshape(D, 3, D)
        norm_one_grad = jnp.dot(qkv_grad, qkv_flat.T, preferred_element_type=jnp.float32)
        gain_one_grad = lax.optimization_barrier(jnp.sum(norm_one_grad * unit_one, axis=0))
        shift_one_grad = lax.optimization_barrier(jnp.sum(norm_one_grad, axis=0))
        row_in_grad = mid_grad + normalize_back(norm_one_grad, unit_one, inverse_one, gain_one)
        sums = (gain_one_grad, shift_one_grad, qkv_weight_grad, qv_grad, proj_weight_grad, proj_offset_grad, gain_two_grad, shift_two_grad, up_weight_grad, up_offset_grad, down_weight_grad, down_offset_grad)
        return (jax.tree.map(jnp.add, carried, sums), (row_out, row_in_grad))
    zeros = (jnp.zeros((D,), jnp.float32), jnp.zeros((D,), jnp.float32), jnp.zeros((D, 3, D), jnp.float32), jnp.zeros((2, H, HD), jnp.float32), jnp.zeros((D, D), jnp.float32), jnp.zeros((D,), jnp.float32), jnp.zeros((D,), jnp.float32), jnp.zeros((D,), jnp.float32), jnp.zeros((D, FF), jnp.float32), jnp.zeros((FF // 128, 128), jnp.float32), jnp.zeros((FF, D), jnp.float32), jnp.zeros((D,), jnp.float32))
    totals, outputs = lax.scan(one_row, zeros, (block_in, segment_ids, out_cotangent))
    block_out, block_in_grad = outputs
    return (block_out, block_in_grad, totals[0], totals[1], totals[2], totals[3], totals[4], totals[5], totals[6], totals[7], totals[8], totals[9], totals[10], totals[11])
```

```python
import jax
import jax.numpy as jnp
from jax import lax
from jax.experimental import pallas as pl
from jax.experimental.pallas import tpu as pltpu
from jax.sharding import PartitionSpec as P

EPSILON = 1e-05
GELU_ROOT = 0.7978845608028654
GELU_CUBIC = 0.044715
SCORE_SCALE = 0.125
NEGATIVE = -1e30


def passed_along(value, axis, steps):
    count = lax.axis_size(axis)
    pairs = [(source, (source + steps) % count) for source in range(count)]
    return lax.ppermute(value, axis, pairs)


def normalize(values, gain_vec, offset):
    center = jnp.mean(values, axis=-1, keepdims=True)
    shifted = values - center
    spread = jnp.mean(shifted * shifted, axis=-1, keepdims=True)
    inverse = lax.rsqrt(spread + EPSILON)
    unit_vals = shifted * inverse
    return (unit_vals, inverse, unit_vals * gain_vec + offset)


def normalize_back(grad_norm, unit_vals, inverse, gain_vec):
    scaled = grad_norm * gain_vec
    mean_first = jnp.mean(scaled, axis=-1, keepdims=True)
    second = jnp.mean(scaled * unit_vals, axis=-1, keepdims=True)
    return inverse * (scaled - mean_first - unit_vals * second)


def gelu_value(pre_gelu):
    return (
        0.5
        * pre_gelu
        * (1.0 + jnp.tanh(GELU_ROOT * (pre_gelu + GELU_CUBIC * pre_gelu * pre_gelu * pre_gelu)))
    )


def gelu_slope(pre_gelu):
    tangent = jnp.tanh(GELU_ROOT * (pre_gelu + GELU_CUBIC * pre_gelu * pre_gelu * pre_gelu))
    return 0.5 * (1.0 + tangent) + 0.5 * pre_gelu * (1.0 - tangent * tangent) * GELU_ROOT * (
        1.0 + 3.0 * GELU_CUBIC * pre_gelu * pre_gelu
    )


def feature_sum(part_sum):
    return lax.psum(part_sum, "tp")


def allowed_pairs(query_pos, query_seg, key_pos, key_seg):
    causal = key_pos[None, :] <= query_pos[:, None]
    same_doc = query_seg[:, :, None] == key_seg[:, None, :]
    return (causal[None] & same_doc)[:, :, None, :]


def pair_grads(query_side, key_side):
    query_vals, query_grad, query_lse, query_delta, query_pos, query_seg = query_side
    key_vals, value_vals, key_pos, key_seg = key_side
    scores = (
        jnp.einsum("rqhd,rkhd->rqhk", query_vals, key_vals, preferred_element_type=jnp.float32)
        * SCORE_SCALE
    )
    allowed = allowed_pairs(query_pos, query_seg, key_pos, key_seg)
    probs = jnp.where(allowed, jnp.exp(scores - query_lse[..., None]), 0.0)
    value_out = jnp.einsum(
        "rqhk,rqhd->rkhd",
        probs.astype(jnp.bfloat16),
        query_grad,
        preferred_element_type=jnp.float32,
    )
    weight_grad = jnp.einsum(
        "rqhd,rkhd->rqhk", query_grad, value_vals, preferred_element_type=jnp.float32
    )
    score_grad = (probs * (weight_grad - query_delta[..., None])).astype(jnp.bfloat16)
    query_out = jnp.einsum(
        "rqhk,rkhd->rqhd", score_grad, key_vals, preferred_element_type=jnp.float32
    )
    key_out = jnp.einsum(
        "rqhk,rqhd->rkhd", score_grad, query_vals, preferred_element_type=jnp.float32
    )
    return (query_out, key_out, value_out)


def body(
    block_in,
    segment_ids,
    out_cotangent,
    attn_gain,
    attn_shift,
    qkv_weight,
    qv_bias,
    proj_weight,
    proj_bias,
    mlp_gain,
    mlp_shift,
    up_weight,
    up_bias,
    down_weight,
    down_bias,
):
    cycle_size = lax.axis_size("ctx")
    cycle_index = lax.axis_index("ctx")
    row_count, row_tokens, model_width = block_in.shape
    piece_len = row_tokens // cycle_size
    token_count = row_count * row_tokens
    gathered = (
        lax.all_gather(attn_gain, "shard", axis=0, tiled=True),
        lax.all_gather(attn_shift, "shard", axis=0, tiled=True),
        lax.all_gather(qkv_weight, "shard", axis=0, tiled=True),
        lax.all_gather(qv_bias, "shard", axis=2, tiled=True),
        lax.all_gather(proj_weight, "shard", axis=1, tiled=True),
        lax.all_gather(proj_bias, "shard", axis=0, tiled=True),
        lax.all_gather(mlp_gain, "shard", axis=0, tiled=True),
        lax.all_gather(mlp_shift, "shard", axis=0, tiled=True),
        lax.all_gather(up_weight, "shard", axis=0, tiled=True),
        lax.all_gather(up_bias, "shard", axis=1, tiled=True),
        lax.all_gather(down_weight, "shard", axis=1, tiled=True),
        lax.all_gather(down_bias, "shard", axis=0, tiled=True),
    )
    (
        gain_one,
        shift_one,
        qkv_full,
        qv_full,
        proj_full,
        proj_offset,
        gain_two,
        shift_two,
        up_full,
        up_offset,
        down_full,
        down_offset,
    ) = gathered
    head_size = qv_full.shape[2]
    head_width = qkv_full.shape[2]
    head_count = head_width // head_size
    all_segments = lax.all_gather(segment_ids, "ctx", axis=1, tiled=True)
    counter = jnp.arange(row_tokens, dtype=jnp.int32)
    local_in, local_cot = (
        lax.all_to_all(block_in, "ctx", split_axis=1, concat_axis=1, tiled=True),
        lax.all_to_all(out_cotangent, "ctx", split_axis=1, concat_axis=1, tiled=True),
    )

    def positions(source):
        return counter // piece_len * row_tokens + source * piece_len + counter % piece_len

    def segments_of(source):
        return jnp.take(all_segments, positions(source), axis=1)

    gain_one_high = gain_one.astype(jnp.float32)
    gain_two_high = gain_two.astype(jnp.float32)
    residual_in = local_in.reshape(token_count, model_width).astype(jnp.float32)
    unit_one, inverse_one, normed = normalize(
        residual_in, gain_one_high, shift_one.astype(jnp.float32)
    )
    normed_one = normed.astype(jnp.bfloat16)
    projected = jnp.einsum("td,dce->tce", normed_one, qkv_full, preferred_element_type=jnp.float32)
    query_bias = qv_full[0].reshape(head_width).astype(jnp.float32)
    value_bias = qv_full[1].reshape(head_width).astype(jnp.float32)
    head_shape = (row_count, row_tokens, head_count, head_size)
    grad_shape = (row_count, row_tokens, head_width)
    pair_shape = (row_count, row_tokens, 2 * head_width)
    queries = (projected[:, 0] + query_bias).astype(jnp.bfloat16).reshape(head_shape)
    key_value = (
        jnp.concatenate([projected[:, 1], projected[:, 2] + value_bias], axis=-1)
        .astype(jnp.bfloat16)
        .reshape(pair_shape)
    )
    own_positions = positions(cycle_index)
    own_segments = segments_of(cycle_index)

    def split_pair(packed):
        return (
            packed[..., :head_width].reshape(head_shape),
            packed[..., head_width:].reshape(head_shape),
        )

    def circle_pass(visit, state):

        def forward_turn(turn_index, carried):
            inner_state, packed = carried
            inner_state = visit(inner_state, packed, (cycle_index - turn_index) % cycle_size)
            packed = passed_along(packed, "ctx", 1)
            return (inner_state, packed)

        state, packed = lax.fori_loop(0, cycle_size - 1, forward_turn, (state, key_value))
        return visit(state, packed, (cycle_index + 1) % cycle_size)

    def block_scores(packed, source):
        key_pos = positions(source)
        key_seg = segments_of(source)
        key_block, value_block = split_pair(packed)
        scores = (
            jnp.einsum("rqhd,rkhd->rqhk", queries, key_block, preferred_element_type=jnp.float32)
            * SCORE_SCALE
        )
        allowed = allowed_pairs(own_positions, own_segments, key_pos, key_seg)
        return (scores, allowed, value_block)

    def reached(source):
        return jnp.min(positions(source)) <= jnp.max(own_positions)

    def gather_stats(softmax_state, packed, source):

        def compute(carried):
            running_max, running_sum = carried
            scores, allowed, value_block = block_scores(packed, source)
            scores = jnp.where(allowed, scores, NEGATIVE)
            new_max = jnp.maximum(running_max, jnp.max(scores, axis=-1))
            weights = jnp.where(allowed, jnp.exp(scores - new_max[..., None]), 0.0)
            running_sum = running_sum * jnp.exp(running_max - new_max) + jnp.sum(weights, axis=-1)
            return (new_max, running_sum)

        return lax.cond(reached(source), compute, lambda carried: carried, softmax_state)

    start_state = (
        jnp.full(head_shape[:3], NEGATIVE, jnp.float32),
        jnp.zeros(head_shape[:3], jnp.float32),
    )
    running_max, running_sum = circle_pass(gather_stats, start_state)
    log_total = running_max + jnp.log(running_sum)

    def gather_mix(accumulated, packed, source):

        def compute(carried):
            scores, allowed, value_block = block_scores(packed, source)
            probs_low = jnp.where(allowed, jnp.exp(scores - log_total[..., None]), 0.0).astype(
                jnp.bfloat16
            )
            return carried + jnp.einsum(
                "rqhk,rkhd->rqhd", probs_low, value_block, preferred_element_type=jnp.float32
            )

        return lax.cond(reached(source), compute, lambda carried: carried, accumulated)

    accumulated = circle_pass(gather_mix, jnp.zeros(head_shape, jnp.float32))
    mixed_heads = accumulated.astype(jnp.bfloat16)
    mixed_flat = mixed_heads.reshape(token_count, head_width)
    residual_mid = (
        residual_in
        + feature_sum(jnp.dot(mixed_flat, proj_full, preferred_element_type=jnp.float32))
        + proj_offset.astype(jnp.float32)
    )
    unit_two, inverse_two, normed = normalize(
        residual_mid, gain_two_high, shift_two.astype(jnp.float32)
    )
    normed_two = normed.astype(jnp.bfloat16)
    pre_gelu = jnp.dot(normed_two, up_full, preferred_element_type=jnp.float32) + up_offset.reshape(
        -1
    ).astype(jnp.float32)
    hidden = gelu_value(pre_gelu).astype(jnp.bfloat16)
    block_out = (
        residual_mid
        + feature_sum(jnp.dot(hidden, down_full, preferred_element_type=jnp.float32))
        + down_offset.astype(jnp.float32)
    )
    cot_low = local_cot.reshape(token_count, model_width)
    cot_high = cot_low.astype(jnp.float32)
    down_offset_grad = jnp.sum(cot_high, axis=0)
    down_weight_grad = jnp.einsum("tf,td->fd", hidden, cot_low, preferred_element_type=jnp.float32)
    pre_grad = jnp.einsum(
        "td,fd->tf", cot_low, down_full, preferred_element_type=jnp.float32
    ) * gelu_slope(pre_gelu)
    up_offset_grad = jnp.sum(pre_grad, axis=0).reshape(up_offset.shape)
    pre_grad_low = pre_grad.astype(jnp.bfloat16)
    up_weight_grad = jnp.einsum(
        "td,tf->df", normed_two, pre_grad_low, preferred_element_type=jnp.float32
    )
    norm_two_grad = feature_sum(
        jnp.einsum("tf,df->td", pre_grad_low, up_full, preferred_element_type=jnp.float32)
    )
    gain_two_grad = jnp.sum(norm_two_grad * unit_two, axis=0)
    shift_two_grad = jnp.sum(norm_two_grad, axis=0)
    mid_grad = cot_high + normalize_back(norm_two_grad, unit_two, inverse_two, gain_two_high)
    proj_offset_grad = jnp.sum(mid_grad, axis=0)
    mid_grad_low = mid_grad.astype(jnp.bfloat16)
    proj_weight_grad = jnp.einsum(
        "te,td->ed", mixed_flat, mid_grad_low, preferred_element_type=jnp.float32
    )
    mixed_grad = (
        jnp.einsum("td,ed->te", mid_grad_low, proj_full, preferred_element_type=jnp.float32)
        .astype(jnp.bfloat16)
        .reshape(head_shape)
    )
    row_delta = jnp.sum(mixed_grad.astype(jnp.float32) * mixed_heads.astype(jnp.float32), axis=-1)
    zero_queries = jnp.zeros(grad_shape, jnp.float32)
    zero_pairs = jnp.zeros(pair_shape, jnp.float32)
    query_side = (queries, mixed_grad, log_total, row_delta, own_positions, own_segments)

    def key_turn(source, packed, carried):
        key_pos = positions(source)
        key_seg = segments_of(source)

        def compute(inputs):
            query_acc, key_acc = inputs
            key_block, value_block = split_pair(packed)
            query_out, key_out, value_out = pair_grads(
                query_side, (key_block, value_block, key_pos, key_seg)
            )
            key_acc = key_acc + jnp.concatenate(
                [key_out.reshape(grad_shape), value_out.reshape(grad_shape)], axis=-1
            )
            return (query_acc + query_out.reshape(grad_shape), key_acc)

        return lax.cond(
            jnp.min(key_pos) <= jnp.max(own_positions), compute, lambda inputs: inputs, carried
        )

    def pass_keys(key_acc):
        return passed_along(key_acc, "ctx", 1)

    def key_back_turn(turn_index, carried):
        packed, query_acc, key_acc = carried
        query_acc, key_acc = key_turn(
            (cycle_index - turn_index) % cycle_size, packed, (query_acc, key_acc)
        )
        packed = passed_along(packed, "ctx", 1)
        return (packed, query_acc, pass_keys(key_acc))

    packed, query_acc, key_acc = lax.fori_loop(
        0, cycle_size - 1, key_back_turn, (key_value, zero_queries, zero_pairs)
    )
    query_acc, key_acc = key_turn((cycle_index + 1) % cycle_size, packed, (query_acc, key_acc))
    key_acc = pass_keys(key_acc)
    query_grad_all = query_acc * SCORE_SCALE
    key_grad_all = key_acc[..., :head_width] * SCORE_SCALE
    value_grad_all = key_acc[..., head_width:]
    qv_grad = jnp.stack(
        [
            jnp.sum(query_grad_all, axis=(0, 1)).reshape(head_count, head_size),
            jnp.sum(value_grad_all, axis=(0, 1)).reshape(head_count, head_size),
        ]
    )
    qkv_grad = (
        jnp.stack([query_grad_all, key_grad_all, value_grad_all], axis=2)
        .astype(jnp.bfloat16)
        .reshape(token_count, 3, head_width)
    )
    qkv_weight_grad = jnp.einsum(
        "td,tce->dce", normed_one, qkv_grad, preferred_element_type=jnp.float32
    )
    norm_one_grad = feature_sum(
        jnp.einsum("tce,dce->td", qkv_grad, qkv_full, preferred_element_type=jnp.float32)
    )
    gain_one_grad = jnp.sum(norm_one_grad * unit_one, axis=0)
    shift_one_grad = jnp.sum(norm_one_grad, axis=0)
    in_grad = mid_grad + normalize_back(norm_one_grad, unit_one, inverse_one, gain_one_high)
    local_grads = (
        gain_one_grad,
        shift_one_grad,
        qkv_weight_grad,
        qv_grad,
        proj_weight_grad,
        proj_offset_grad,
        gain_two_grad,
        shift_two_grad,
        up_weight_grad,
        up_offset_grad,
        down_weight_grad,
        down_offset_grad,
    )
    owned = (
        lax.psum_scatter(local_grads[0], "shard", scatter_dimension=0, tiled=True),
        lax.psum_scatter(local_grads[1], "shard", scatter_dimension=0, tiled=True),
        lax.psum_scatter(local_grads[2], "shard", scatter_dimension=0, tiled=True),
        lax.psum_scatter(local_grads[3], "shard", scatter_dimension=2, tiled=True),
        lax.psum_scatter(local_grads[4], "shard", scatter_dimension=1, tiled=True),
        lax.psum_scatter(local_grads[5], "shard", scatter_dimension=0, tiled=True),
        lax.psum_scatter(local_grads[6], "shard", scatter_dimension=0, tiled=True),
        lax.psum_scatter(local_grads[7], "shard", scatter_dimension=0, tiled=True),
        lax.psum_scatter(local_grads[8], "shard", scatter_dimension=0, tiled=True),
        lax.psum_scatter(local_grads[9], "shard", scatter_dimension=1, tiled=True),
        lax.psum_scatter(local_grads[10], "shard", scatter_dimension=1, tiled=True),
        lax.psum_scatter(local_grads[11], "shard", scatter_dimension=0, tiled=True),
    )
    totals = lax.psum(
        (
            owned[0],
            owned[1],
            owned[2],
            owned[3],
            owned[4],
            owned[5],
            owned[6],
            owned[7],
            owned[8],
            owned[9],
            owned[10],
            owned[11],
        ),
        "ctx",
    )
    block_out = block_out.reshape(row_count, row_tokens, model_width)
    in_grad = in_grad.reshape(row_count, row_tokens, model_width)
    block_out, in_grad = (
        lax.all_to_all(block_out, "ctx", split_axis=1, concat_axis=1, tiled=True),
        lax.all_to_all(in_grad, "ctx", split_axis=1, concat_axis=1, tiled=True),
    )
    return (block_out, in_grad) + tuple(totals)


MESH = pl.DeviceIdType.MESH
F32 = jnp.float32
BF16 = jnp.bfloat16
GAIN_ONE, SHIFT_ONE, PROJ_BIAS, GAIN_TWO, SHIFT_TWO, DOWN_BIAS, UP_BIAS, Q_BIAS, V_BIAS = range(9)
VEC_ROWS = 16
COPIES = 64


def mm(left, right, dims=((1,), (0,))):
    return lax.dot_general(left, right, (dims, ((), ())), preferred_element_type=F32)


NT = ((1,), (1,))
TN = ((0,), (0,))


def block_kernel(
    x_ref, cot_ref, segq_ref, segk_ref, attn_w, up_w, down_w, vec_ref,
    out_ref, in_grad_ref, attn_g_ref, up_g_ref, down_g_ref, vec_g_ref,
    attn_f, up_f, down_f, vec_in, segk_in, kv, kv_in, dkv, dkv_in,
    part, ar_send, ar_recv, ar_all,
    attn_g, up_g, down_g, attn_s1, attn_r1, attn_s2, attn_r2, attn_s3, attn_r3,
    mlp_s1, mlp_r1, mlp_s2, mlp_r2, mlp_s3, mlp_r3,
    vec_s, vec_r, send_sem, recv_sem,
):
    shard = lax.axis_index("shard")
    ctx = lax.axis_index("ctx")
    tp = lax.axis_index("tp")
    core = lax.rem(shard, 2)
    high = shard // 2
    s1 = shard + 1 - 2 * core
    s2 = lax.rem(shard + 2, 4)
    s3 = lax.rem(s1 + 2, 4)
    p1, p2, p3 = {"shard": s1}, {"shard": s2}, {"shard": s3}
    pc = {"ctx": 1 - ctx}
    tps = [lax.rem(tp + step, 4) for step in (1, 2, 3)]
    tokens, width = x_ref.shape
    depth = up_w.shape[0]
    heads_width = attn_w.shape[2]
    head_count = heads_width // 64

    barrier = pltpu.get_barrier_semaphore()
    peers = [p1, p2, p3, pc] + [{"tp": t} for t in tps]
    for peer in peers:
        pl.semaphore_signal(barrier, inc=1, device_id=peer, device_id_type=MESH)

    started = []

    def send(src, dst, peer):
        slot = len(started)
        copy = pltpu.make_async_remote_copy(
            src_ref=src, dst_ref=dst, send_sem=send_sem.at[slot], recv_sem=recv_sem.at[slot],
            device_id=peer, device_id_type=MESH,
        )
        copy.start()
        started.append(copy)
        return copy

    def unit_of(values):
        center = jnp.mean(values, axis=-1, keepdims=True)
        shifted = values - center
        inverse = lax.rsqrt(jnp.mean(shifted * shifted, axis=-1, keepdims=True) + EPSILON)
        return shifted * inverse, inverse

    pl.semaphore_wait(barrier, len(peers))

    def gather_start(local, full):
        far = send(local, full.at[shard], p2)
        near = send(local, full.at[shard], p1)
        return far, near

    def gather_pass(full, far):
        far.wait_recv()
        return send(full.at[s2], full.at[s2], p1)

    attn_far, attn_near = gather_start(attn_w, attn_f)
    vec_copies = [send(vec_ref, vec_in.at[i], p) for i, p in enumerate((p1, p2, p3))]
    seg_copy = send(segk_ref, segk_in, pc)
    attn_f[shard] = attn_w[...]
    up_f[shard] = up_w[...]
    down_f[shard] = down_w[...]
    residual_in = x_ref[...].astype(F32)
    unit_one, inverse_one = unit_of(residual_in)
    for copy in vec_copies:
        copy.wait_recv()
    vec = vec_ref[...] + vec_in[0] + vec_in[1] + vec_in[2]

    def row(index, size=width):
        return vec[index : index + 1, :size]

    normed_one = (unit_one * row(GAIN_ONE) + row(SHIFT_ONE)).astype(BF16)
    attn_pass = gather_pass(attn_f, attn_far)
    up_far, up_near = gather_start(up_w, up_f)
    down_far, down_near = gather_start(down_w, down_f)
    attn_near.wait_recv()
    attn_pass.wait_recv()
    weight_q, weight_k, weight_v, weight_p = (
        attn_f[:, index].reshape(4 * depth, heads_width) for index in range(4)
    )
    keys = mm(normed_one, weight_k).astype(BF16)
    values = (mm(normed_one, weight_v) + row(V_BIAS, heads_width)).astype(BF16)
    kv[0] = keys
    kv[1] = values
    kv_copy = send(kv, kv_in, pc)
    queries = (mm(normed_one, weight_q) + row(Q_BIAS, heads_width)).astype(BF16)

    lane_head = lax.broadcasted_iota(jnp.int32, (tokens, heads_width), 1) // 64
    of_head = [lane_head == index for index in range(head_count)]

    def pick(values_in, index):
        return jnp.where(of_head[index], values_in, jnp.zeros_like(values_in))

    seg_copy.wait_recv()
    query_at = lax.broadcasted_iota(jnp.int32, (tokens, tokens), 0)
    key_at = lax.broadcasted_iota(jnp.int32, (tokens, tokens), 1)
    segq = segq_ref[...]
    allow_own = (key_at <= query_at) & (segq == segk_ref[0:1, :])
    allow_other = (segq == segk_in[0:1, :]) & (key_at + tokens * (1 - ctx) <= query_at + tokens * ctx)
    query_of = [pick(queries, index) for index in range(head_count)]
    score_own = [
        jnp.where(allow_own, mm(query_of[i], keys, NT) * SCORE_SCALE, NEGATIVE)
        for i in range(head_count)
    ]
    kv_copy.wait_recv()
    keys_other = kv_in[0]
    values_other = kv_in[1]
    probs_own, probs_other = [], []
    mixed_sum = jnp.zeros((tokens, heads_width), F32)
    for i in range(head_count):
        own = score_own[i]
        other = jnp.where(allow_other, mm(query_of[i], keys_other, NT) * SCORE_SCALE, NEGATIVE)
        top = jnp.maximum(
            jnp.max(own, axis=-1, keepdims=True), jnp.max(other, axis=-1, keepdims=True)
        )
        total = jnp.sum(jnp.exp(own - top), axis=-1, keepdims=True) + jnp.sum(
            jnp.exp(other - top), axis=-1, keepdims=True
        )
        log_total = top + jnp.log(total)
        probs_own.append(jnp.where(allow_own, jnp.exp(own - log_total), 0.0))
        probs_other.append(jnp.where(allow_other, jnp.exp(other - log_total), 0.0))
        mixed_head = mm(probs_own[i].astype(BF16), values) + mm(
            probs_other[i].astype(BF16), values_other
        )
        mixed_sum = mixed_sum + pick(mixed_head, i)
    mixed = mixed_sum.astype(BF16)

    def sum_start(phase, value):
        pieces = value.reshape(4, tokens // 4, width)
        part[phase] = pieces
        ar_send[phase] = pieces.astype(BF16)
        return [send(ar_send.at[phase, t], ar_recv.at[phase, i], {"tp": t}) for i, t in enumerate(tps)]

    def sum_pass(phase, copies):
        total = part[phase, tp]
        for i, copy in enumerate(copies):
            copy.wait_recv()
            total = total + ar_recv[phase, i].astype(F32)
        ar_all[phase, tp] = total.astype(BF16)
        return [send(ar_all.at[phase, tp], ar_all.at[phase, tp], {"tp": t}) for t in tps]

    def sum_end(phase, copies):
        for copy in copies:
            copy.wait_recv()
        return ar_all[phase].reshape(tokens, width).astype(F32)

    mid_sum = sum_start(0, mm(mixed, weight_p, NT))
    up_pass = gather_pass(up_f, up_far)
    mid_sum = sum_pass(0, mid_sum)
    down_pass = gather_pass(down_f, down_far)
    residual_mid = residual_in + sum_end(0, mid_sum) + row(PROJ_BIAS)
    unit_two, inverse_two = unit_of(residual_mid)
    normed_two = (unit_two * row(GAIN_TWO) + row(SHIFT_TWO)).astype(BF16)
    up_near.wait_recv()
    up_pass.wait_recv()
    up_full = up_f[...].reshape(4 * depth, up_f.shape[2])
    pre_gelu = mm(normed_two, up_full) + row(UP_BIAS)
    tangent = jnp.tanh(GELU_ROOT * (pre_gelu + GELU_CUBIC * pre_gelu * pre_gelu * pre_gelu))
    hidden = (0.5 * pre_gelu * (1.0 + tangent)).astype(BF16)
    slope = 0.5 * (1.0 + tangent) + 0.5 * pre_gelu * (1.0 - tangent * tangent) * GELU_ROOT * (
        1.0 + 3.0 * GELU_CUBIC * pre_gelu * pre_gelu
    )
    down_near.wait_recv()
    down_pass.wait_recv()
    down_full = down_f[...].reshape(4 * depth, down_f.shape[2])
    cot_low = cot_ref[...]
    cot_high = cot_low.astype(F32)
    pre_grad = mm(cot_low, down_full) * slope
    pre_grad_low = pre_grad.astype(BF16)
    two_sum = sum_start(2, mm(pre_grad_low, up_full, NT))
    out_sum = sum_start(1, mm(hidden, down_full, NT))

    def column_sum(value):
        return jnp.sum(value, axis=0, keepdims=True)

    vec_s[0] = jnp.zeros((VEC_ROWS, width), F32)
    vec_s[0, UP_BIAS : UP_BIAS + 1, :] = column_sum(pre_grad)
    vec_s[0, DOWN_BIAS : DOWN_BIAS + 1, :] = column_sum(cot_high)

    def reduce_one(grads, s1_buf, r1_buf):
        for half in range(2):
            s1_buf[half] = grads[2 * half + 1 - core].astype(BF16)
        return send(s1_buf, r1_buf, p1)

    def reduce_two(copy, grads, r1_buf, s2_buf, r2_buf):
        copy.wait_recv()
        s2_buf[...] = (grads[s2] + r1_buf[1 - high].astype(F32)).astype(BF16)
        return send(s2_buf, r2_buf, p2)

    def reduce_three(copy, grads, r1_buf, r2_buf, s3_buf, r3_buf):
        copy.wait_recv()
        s3_buf[...] = (
            grads[shard] + r1_buf[high].astype(F32) + r2_buf[...].astype(F32)
        ).astype(BF16)
        return send(s3_buf, r3_buf, pc)

    def reduce_end(copy, s3_buf, r3_buf, result):
        copy.wait_recv()
        result[...] = s3_buf[...].astype(F32) + r3_buf[...].astype(F32)

    down_g[...] = mm(cot_low, hidden, TN).reshape(down_g.shape)
    down_copy = reduce_one(down_g, mlp_s1.at[1], mlp_r1.at[1])
    two_sum = sum_pass(2, two_sum)
    up_g[...] = mm(normed_two, pre_grad_low, TN).reshape(up_g.shape)
    up_copy = reduce_one(up_g, mlp_s1.at[0], mlp_r1.at[0])
    down_copy = reduce_two(down_copy, down_g, mlp_r1.at[1], mlp_s2.at[1], mlp_r2.at[1])
    norm_two_grad = sum_end(2, two_sum)
    vec_s[0, GAIN_TWO : GAIN_TWO + 1, :] = column_sum(norm_two_grad * unit_two)
    vec_s[0, SHIFT_TWO : SHIFT_TWO + 1, :] = column_sum(norm_two_grad)
    mid_grad = cot_high + normalize_back(norm_two_grad, unit_two, inverse_two, row(GAIN_TWO))
    vec_s[0, PROJ_BIAS : PROJ_BIAS + 1, :] = column_sum(mid_grad)
    mid_grad_low = mid_grad.astype(BF16)
    mixed_grad = mm(mid_grad_low, weight_p).astype(BF16)
    delta_terms = mixed_grad.astype(F32) * mixed.astype(F32)
    zero = jnp.zeros((tokens, heads_width), F32)
    query_grad, key_own, value_own, key_other, value_other = zero, zero, zero, zero, zero
    for i in range(head_count):
        head_grad = pick(mixed_grad, i)
        delta = jnp.sum(pick(delta_terms, i), axis=-1, keepdims=True)
        grad_other = (probs_other[i] * (mm(head_grad, values_other, NT) - delta)).astype(BF16)
        grad_own = (probs_own[i] * (mm(head_grad, values, NT) - delta)).astype(BF16)
        key_other = key_other + mm(grad_other, query_of[i], TN)
        value_other = value_other + mm(probs_other[i].astype(BF16), head_grad, TN)
        key_own = key_own + mm(grad_own, query_of[i], TN)
        value_own = value_own + mm(probs_own[i].astype(BF16), head_grad, TN)
        query_grad = query_grad + pick(mm(grad_own, keys) + mm(grad_other, keys_other), i)
    dkv[0] = key_other.astype(BF16)
    dkv[1] = value_other.astype(BF16)
    dkv_copy = send(dkv, dkv_in, pc)
    up_copy = reduce_two(up_copy, up_g, mlp_r1.at[0], mlp_s2.at[0], mlp_r2.at[0])
    out_sum = sum_pass(1, out_sum)
    proj_grad = mm(mid_grad_low, mixed, TN).reshape(4, depth, heads_width)
    for index in range(4):
        attn_g[index, 3] = proj_grad[index]
    query_grad = query_grad * SCORE_SCALE
    query_low = query_grad.astype(BF16)
    vec_s[0, Q_BIAS : Q_BIAS + 1, :heads_width] = column_sum(query_grad)
    one_part = mm(query_low, weight_q, NT)
    dkv_copy.wait_recv()
    key_low = ((key_own + dkv_in[0].astype(F32)) * SCORE_SCALE).astype(BF16)
    value_grad = value_own + dkv_in[1].astype(F32)
    value_low = value_grad.astype(BF16)
    vec_s[0, V_BIAS : V_BIAS + 1, :heads_width] = column_sum(value_grad)
    one_part = one_part + mm(key_low, weight_k, NT) + mm(value_low, weight_v, NT)
    one_sum = sum_start(3, one_part)
    for index, grad_low in enumerate((query_low, key_low, value_low)):
        weight_grad = mm(normed_one, grad_low, TN).reshape(4, depth, heads_width)
        for block in range(4):
            attn_g[block, index] = weight_grad[block]
    attn_copy = reduce_one(attn_g, attn_s1, attn_r1)
    one_sum = sum_pass(3, one_sum)
    attn_copy = reduce_two(attn_copy, attn_g, attn_r1, attn_s2, attn_r2)
    down_copy = reduce_three(
        down_copy, down_g, mlp_r1.at[1], mlp_r2.at[1], mlp_s3.at[1], mlp_r3.at[1]
    )
    up_copy = reduce_three(up_copy, up_g, mlp_r1.at[0], mlp_r2.at[0], mlp_s3.at[0], mlp_r3.at[0])
    norm_one_grad = sum_end(3, one_sum)
    vec_s[0, GAIN_ONE : GAIN_ONE + 1, :] = column_sum(norm_one_grad * unit_one)
    vec_s[0, SHIFT_ONE : SHIFT_ONE + 1, :] = column_sum(norm_one_grad)
    vec_copy = send(vec_s.at[0], vec_r.at[0], p1)
    attn_copy = reduce_three(attn_copy, attn_g, attn_r1, attn_r2, attn_s3, attn_r3)
    in_grad_ref[...] = mid_grad + normalize_back(
        norm_one_grad, unit_one, inverse_one, row(GAIN_ONE)
    )
    vec_copy.wait_recv()
    vec_s[1] = vec_s[0] + vec_r[0]
    vec_copy = send(vec_s.at[1], vec_r.at[1], p2)
    out_ref[...] = residual_mid + sum_end(1, out_sum) + row(DOWN_BIAS)
    vec_copy.wait_recv()
    vec_s[2] = vec_s[1] + vec_r[1]
    vec_copy = send(vec_s.at[2], vec_r.at[2], pc)
    reduce_end(down_copy, mlp_s3.at[1], mlp_r3.at[1], down_g_ref)
    reduce_end(up_copy, mlp_s3.at[0], mlp_r3.at[0], up_g_ref)
    reduce_end(attn_copy, attn_s3, attn_r3, attn_g_ref)
    vec_copy.wait_recv()
    vec_g_ref[...] = vec_s[2] + vec_r[2]
    for copy in started:
        copy.wait_send()


def paired_body(
    block_in, segment_ids, out_cotangent, attn_gain, attn_shift, qkv_weight, qv_bias, proj_weight,
    proj_bias, mlp_gain, mlp_shift, up_weight, up_bias, down_weight, down_bias,
):
    shard = lax.axis_index("shard")
    shards = lax.axis_size("shard")
    _, tokens, width = block_in.shape
    depth = qkv_weight.shape[0]
    heads_width = qkv_weight.shape[2]
    units = up_weight.shape[1]
    head_count, head_piece = qv_bias.shape[1:]
    up_rows, up_piece = up_bias.shape
    wide = jnp.stack([attn_gain, attn_shift, proj_bias, mlp_gain, mlp_shift, down_bias]).astype(F32)

    def placed(value):
        axis = value.ndim - 1
        size = value.shape[axis]
        room = jnp.zeros(value.shape[:-1] + (size * shards,), F32)
        return lax.dynamic_update_slice_in_dim(room, value, shard * size, axis)

    wide = placed(wide)
    up_row = placed(up_bias.astype(F32)).reshape(1, units)
    qv_rows = placed(qv_bias.astype(F32)).reshape(2, heads_width)
    qv_rows = jnp.pad(qv_rows, ((0, VEC_ROWS - 9), (0, width - heads_width)))
    vec = jnp.concatenate([wide, up_row, qv_rows], axis=0)
    attn_w = jnp.concatenate(
        [jnp.transpose(qkv_weight, (1, 0, 2)), jnp.transpose(proj_weight)[None]], axis=0
    )
    segq = jnp.broadcast_to(segment_ids.reshape(tokens, 1), (tokens, tokens))
    segk = jnp.broadcast_to(segment_ids.reshape(1, tokens), (8, tokens))
    attn_shape = (4, depth, heads_width)
    mlp_shape = (depth, units)
    vmem = pltpu.VMEM
    out_shapes = (
        jax.ShapeDtypeStruct((tokens, width), F32),
        jax.ShapeDtypeStruct((tokens, width), F32),
        jax.ShapeDtypeStruct(attn_shape, F32),
        jax.ShapeDtypeStruct(mlp_shape, F32),
        jax.ShapeDtypeStruct(mlp_shape, F32),
        jax.ShapeDtypeStruct((VEC_ROWS, width), F32),
    )
    scratch = [
        vmem((4,) + attn_shape, BF16), vmem((4,) + mlp_shape, BF16), vmem((4,) + mlp_shape, BF16),
        vmem((3, VEC_ROWS, width), F32), vmem((8, tokens), jnp.int32),
        vmem((2, tokens, heads_width), BF16), vmem((2, tokens, heads_width), BF16),
        vmem((2, tokens, heads_width), BF16), vmem((2, tokens, heads_width), BF16),
        vmem((4, 4, tokens // 4, width), F32), vmem((4, 4, tokens // 4, width), BF16),
        vmem((4, 3, tokens // 4, width), BF16), vmem((4, 4, tokens // 4, width), BF16),
        vmem((4,) + attn_shape, F32), vmem((4,) + mlp_shape, F32), vmem((4,) + mlp_shape, F32),
        vmem((2,) + attn_shape, BF16), vmem((2,) + attn_shape, BF16),
        vmem(attn_shape, BF16), vmem(attn_shape, BF16), vmem(attn_shape, BF16), vmem(attn_shape, BF16),
        vmem((2, 2) + mlp_shape, BF16), vmem((2, 2) + mlp_shape, BF16),
        vmem((2,) + mlp_shape, BF16), vmem((2,) + mlp_shape, BF16),
        vmem((2,) + mlp_shape, BF16), vmem((2,) + mlp_shape, BF16),
        vmem((3, VEC_ROWS, width), F32), vmem((3, VEC_ROWS, width), F32),
        pltpu.SemaphoreType.DMA((COPIES,)), pltpu.SemaphoreType.DMA((COPIES,)),
    ]
    whole = pl.BlockSpec(memory_space=pltpu.VMEM)
    block_out, in_grad, attn_g, up_g, down_g, vec_g = pl.pallas_call(
        block_kernel,
        out_shape=out_shapes,
        in_specs=[whole] * 8,
        out_specs=(whole,) * 6,
        scratch_shapes=scratch,
        compiler_params=pltpu.CompilerParams(
            collective_id=0, has_side_effects=True, vmem_limit_bytes=56 * 1024 * 1024
        ),
    )(
        block_in[0], out_cotangent[0], segq, segk, attn_w, up_weight, jnp.transpose(down_weight), vec
    )
    mine = lax.dynamic_slice_in_dim(vec_g[:6], shard * depth, depth, 1)
    up_b = lax.dynamic_slice_in_dim(
        vec_g[UP_BIAS].reshape(up_rows, up_piece * shards), shard * up_piece, up_piece, 1
    )
    qv_b = lax.dynamic_slice_in_dim(
        vec_g[Q_BIAS : V_BIAS + 1, :heads_width].reshape(2, head_count, head_piece * shards),
        shard * head_piece, head_piece, 2,
    )
    return (
        block_out[None], in_grad[None], mine[0], mine[1], jnp.transpose(attn_g[:3], (1, 0, 2)), qv_b,
        jnp.transpose(attn_g[3]), mine[2], mine[3], mine[4], up_g, up_b, jnp.transpose(down_g), mine[5],
    )


def solution(mesh):
    paired = mesh.shape["ctx"] == 2 and mesh.shape["shard"] == 4 and mesh.shape["tp"] == 4
    return jax.shard_map(
        paired_body if paired else body,
        mesh=mesh,
        in_specs=(
            P("shard", "ctx", None),
            P("shard", "ctx"),
            P("shard", "ctx", None),
            P("shard"),
            P("shard"),
            P("shard", None, "tp"),
            P(None, "tp", "shard"),
            P("tp", "shard"),
            P("shard"),
            P("shard"),
            P("shard"),
            P("shard", "tp"),
            P("tp", "shard"),
            P("tp", "shard"),
            P("shard"),
        ),
        out_specs=(
            P("shard", "ctx", None),
            P("shard", "ctx", None),
            P("shard"),
            P("shard"),
            P("shard", None, "tp"),
            P(None, "tp", "shard"),
            P("tp", "shard"),
            P("shard"),
            P("shard"),
            P("shard"),
            P("shard", "tp"),
            P("tp", "shard"),
            P("tp", "shard"),
            P("shard"),
        ),
        check_vma=False,
    )
```

```python
import jax
import jax.numpy as jnp
from jax import lax
from jax.experimental import pallas as pl
from jax.experimental.pallas import tpu as pltpu
from jax.sharding import PartitionSpec as P

EPSILON = 1e-05
GELU_ROOT = 0.7978845608028654
GELU_CUBIC = 0.044715
SCORE_SCALE = 0.125
NEGATIVE = -1e30


def passed_along(value, axis, steps):
    count = lax.axis_size(axis)
    pairs = [(source, (source + steps) % count) for source in range(count)]
    return lax.ppermute(value, axis, pairs)


def normalize(values, gain_vec, offset):
    center = jnp.mean(values, axis=-1, keepdims=True)
    shifted = values - center
    spread = jnp.mean(shifted * shifted, axis=-1, keepdims=True)
    inverse = lax.rsqrt(spread + EPSILON)
    unit_vals = shifted * inverse
    return (unit_vals, inverse, unit_vals * gain_vec + offset)


def normalize_back(grad_norm, unit_vals, inverse, gain_vec):
    scaled = grad_norm * gain_vec
    mean_first = jnp.mean(scaled, axis=-1, keepdims=True)
    second = jnp.mean(scaled * unit_vals, axis=-1, keepdims=True)
    return inverse * (scaled - mean_first - unit_vals * second)


def gelu_value(pre_gelu):
    return (
        0.5
        * pre_gelu
        * (1.0 + jnp.tanh(GELU_ROOT * (pre_gelu + GELU_CUBIC * pre_gelu * pre_gelu * pre_gelu)))
    )


def gelu_slope(pre_gelu):
    tangent = jnp.tanh(GELU_ROOT * (pre_gelu + GELU_CUBIC * pre_gelu * pre_gelu * pre_gelu))
    return 0.5 * (1.0 + tangent) + 0.5 * pre_gelu * (1.0 - tangent * tangent) * GELU_ROOT * (
        1.0 + 3.0 * GELU_CUBIC * pre_gelu * pre_gelu
    )


def feature_sum(part_sum):
    return lax.psum(part_sum, "tp")


def allowed_pairs(query_pos, query_seg, key_pos, key_seg):
    causal = key_pos[None, :] <= query_pos[:, None]
    same_doc = query_seg[:, :, None] == key_seg[:, None, :]
    return (causal[None] & same_doc)[:, :, None, :]


def pair_grads(query_side, key_side):
    query_vals, query_grad, query_lse, query_delta, query_pos, query_seg = query_side
    key_vals, value_vals, key_pos, key_seg = key_side
    scores = (
        jnp.einsum("rqhd,rkhd->rqhk", query_vals, key_vals, preferred_element_type=jnp.float32)
        * SCORE_SCALE
    )
    allowed = allowed_pairs(query_pos, query_seg, key_pos, key_seg)
    probs = jnp.where(allowed, jnp.exp(scores - query_lse[..., None]), 0.0)
    value_out = jnp.einsum(
        "rqhk,rqhd->rkhd",
        probs.astype(jnp.bfloat16),
        query_grad,
        preferred_element_type=jnp.float32,
    )
    weight_grad = jnp.einsum(
        "rqhd,rkhd->rqhk", query_grad, value_vals, preferred_element_type=jnp.float32
    )
    score_grad = (probs * (weight_grad - query_delta[..., None])).astype(jnp.bfloat16)
    query_out = jnp.einsum(
        "rqhk,rkhd->rqhd", score_grad, key_vals, preferred_element_type=jnp.float32
    )
    key_out = jnp.einsum(
        "rqhk,rqhd->rkhd", score_grad, query_vals, preferred_element_type=jnp.float32
    )
    return (query_out, key_out, value_out)


def body(
    block_in,
    segment_ids,
    out_cotangent,
    attn_gain,
    attn_shift,
    qkv_weight,
    qv_bias,
    proj_weight,
    proj_bias,
    mlp_gain,
    mlp_shift,
    up_weight,
    up_bias,
    down_weight,
    down_bias,
):
    cycle_size = lax.axis_size("ctx")
    cycle_index = lax.axis_index("ctx")
    row_count, row_tokens, model_width = block_in.shape
    piece_len = row_tokens // cycle_size
    token_count = row_count * row_tokens
    gathered = (
        lax.all_gather(attn_gain, "shard", axis=0, tiled=True),
        lax.all_gather(attn_shift, "shard", axis=0, tiled=True),
        lax.all_gather(qkv_weight, "shard", axis=0, tiled=True),
        lax.all_gather(qv_bias, "shard", axis=2, tiled=True),
        lax.all_gather(proj_weight, "shard", axis=1, tiled=True),
        lax.all_gather(proj_bias, "shard", axis=0, tiled=True),
        lax.all_gather(mlp_gain, "shard", axis=0, tiled=True),
        lax.all_gather(mlp_shift, "shard", axis=0, tiled=True),
        lax.all_gather(up_weight, "shard", axis=0, tiled=True),
        lax.all_gather(up_bias, "shard", axis=1, tiled=True),
        lax.all_gather(down_weight, "shard", axis=1, tiled=True),
        lax.all_gather(down_bias, "shard", axis=0, tiled=True),
    )
    (
        gain_one,
        shift_one,
        qkv_full,
        qv_full,
        proj_full,
        proj_offset,
        gain_two,
        shift_two,
        up_full,
        up_offset,
        down_full,
        down_offset,
    ) = gathered
    head_size = qv_full.shape[2]
    head_width = qkv_full.shape[2]
    head_count = head_width // head_size
    all_segments = lax.all_gather(segment_ids, "ctx", axis=1, tiled=True)
    counter = jnp.arange(row_tokens, dtype=jnp.int32)
    local_in, local_cot = (
        lax.all_to_all(block_in, "ctx", split_axis=1, concat_axis=1, tiled=True),
        lax.all_to_all(out_cotangent, "ctx", split_axis=1, concat_axis=1, tiled=True),
    )

    def positions(source):
        return counter // piece_len * row_tokens + source * piece_len + counter % piece_len

    def segments_of(source):
        return jnp.take(all_segments, positions(source), axis=1)

    gain_one_high = gain_one.astype(jnp.float32)
    gain_two_high = gain_two.astype(jnp.float32)
    residual_in = local_in.reshape(token_count, model_width).astype(jnp.float32)
    unit_one, inverse_one, normed = normalize(
        residual_in, gain_one_high, shift_one.astype(jnp.float32)
    )
    normed_one = normed.astype(jnp.bfloat16)
    projected = jnp.einsum("td,dce->tce", normed_one, qkv_full, preferred_element_type=jnp.float32)
    query_bias = qv_full[0].reshape(head_width).astype(jnp.float32)
    value_bias = qv_full[1].reshape(head_width).astype(jnp.float32)
    head_shape = (row_count, row_tokens, head_count, head_size)
    grad_shape = (row_count, row_tokens, head_width)
    pair_shape = (row_count, row_tokens, 2 * head_width)
    queries = (projected[:, 0] + query_bias).astype(jnp.bfloat16).reshape(head_shape)
    key_value = (
        jnp.concatenate([projected[:, 1], projected[:, 2] + value_bias], axis=-1)
        .astype(jnp.bfloat16)
        .reshape(pair_shape)
    )
    own_positions = positions(cycle_index)
    own_segments = segments_of(cycle_index)

    def split_pair(packed):
        return (
            packed[..., :head_width].reshape(head_shape),
            packed[..., head_width:].reshape(head_shape),
        )

    def circle_pass(visit, state):

        def forward_turn(turn_index, carried):
            inner_state, packed = carried
            inner_state = visit(inner_state, packed, (cycle_index - turn_index) % cycle_size)
            packed = passed_along(packed, "ctx", 1)
            return (inner_state, packed)

        state, packed = lax.fori_loop(0, cycle_size - 1, forward_turn, (state, key_value))
        return visit(state, packed, (cycle_index + 1) % cycle_size)

    def block_scores(packed, source):
        key_pos = positions(source)
        key_seg = segments_of(source)
        key_block, value_block = split_pair(packed)
        scores = (
            jnp.einsum("rqhd,rkhd->rqhk", queries, key_block, preferred_element_type=jnp.float32)
            * SCORE_SCALE
        )
        allowed = allowed_pairs(own_positions, own_segments, key_pos, key_seg)
        return (scores, allowed, value_block)

    def reached(source):
        return jnp.min(positions(source)) <= jnp.max(own_positions)

    def gather_stats(softmax_state, packed, source):

        def compute(carried):
            running_max, running_sum = carried
            scores, allowed, value_block = block_scores(packed, source)
            scores = jnp.where(allowed, scores, NEGATIVE)
            new_max = jnp.maximum(running_max, jnp.max(scores, axis=-1))
            weights = jnp.where(allowed, jnp.exp(scores - new_max[..., None]), 0.0)
            running_sum = running_sum * jnp.exp(running_max - new_max) + jnp.sum(weights, axis=-1)
            return (new_max, running_sum)

        return lax.cond(reached(source), compute, lambda carried: carried, softmax_state)

    start_state = (
        jnp.full(head_shape[:3], NEGATIVE, jnp.float32),
        jnp.zeros(head_shape[:3], jnp.float32),
    )
    running_max, running_sum = circle_pass(gather_stats, start_state)
    log_total = running_max + jnp.log(running_sum)

    def gather_mix(accumulated, packed, source):

        def compute(carried):
            scores, allowed, value_block = block_scores(packed, source)
            probs_low = jnp.where(allowed, jnp.exp(scores - log_total[..., None]), 0.0).astype(
                jnp.bfloat16
            )
            return carried + jnp.einsum(
                "rqhk,rkhd->rqhd", probs_low, value_block, preferred_element_type=jnp.float32
            )

        return lax.cond(reached(source), compute, lambda carried: carried, accumulated)

    accumulated = circle_pass(gather_mix, jnp.zeros(head_shape, jnp.float32))
    mixed_heads = accumulated.astype(jnp.bfloat16)
    mixed_flat = mixed_heads.reshape(token_count, head_width)
    residual_mid = (
        residual_in
        + feature_sum(jnp.dot(mixed_flat, proj_full, preferred_element_type=jnp.float32))
        + proj_offset.astype(jnp.float32)
    )
    unit_two, inverse_two, normed = normalize(
        residual_mid, gain_two_high, shift_two.astype(jnp.float32)
    )
    normed_two = normed.astype(jnp.bfloat16)
    pre_gelu = jnp.dot(normed_two, up_full, preferred_element_type=jnp.float32) + up_offset.reshape(
        -1
    ).astype(jnp.float32)
    hidden = gelu_value(pre_gelu).astype(jnp.bfloat16)
    block_out = (
        residual_mid
        + feature_sum(jnp.dot(hidden, down_full, preferred_element_type=jnp.float32))
        + down_offset.astype(jnp.float32)
    )
    cot_low = local_cot.reshape(token_count, model_width)
    cot_high = cot_low.astype(jnp.float32)
    down_offset_grad = jnp.sum(cot_high, axis=0)
    down_weight_grad = jnp.einsum("tf,td->fd", hidden, cot_low, preferred_element_type=jnp.float32)
    pre_grad = jnp.einsum(
        "td,fd->tf", cot_low, down_full, preferred_element_type=jnp.float32
    ) * gelu_slope(pre_gelu)
    up_offset_grad = jnp.sum(pre_grad, axis=0).reshape(up_offset.shape)
    pre_grad_low = pre_grad.astype(jnp.bfloat16)
    up_weight_grad = jnp.einsum(
        "td,tf->df", normed_two, pre_grad_low, preferred_element_type=jnp.float32
    )
    norm_two_grad = feature_sum(
        jnp.einsum("tf,df->td", pre_grad_low, up_full, preferred_element_type=jnp.float32)
    )
    gain_two_grad = jnp.sum(norm_two_grad * unit_two, axis=0)
    shift_two_grad = jnp.sum(norm_two_grad, axis=0)
    mid_grad = cot_high + normalize_back(norm_two_grad, unit_two, inverse_two, gain_two_high)
    proj_offset_grad = jnp.sum(mid_grad, axis=0)
    mid_grad_low = mid_grad.astype(jnp.bfloat16)
    proj_weight_grad = jnp.einsum(
        "te,td->ed", mixed_flat, mid_grad_low, preferred_element_type=jnp.float32
    )
    mixed_grad = (
        jnp.einsum("td,ed->te", mid_grad_low, proj_full, preferred_element_type=jnp.float32)
        .astype(jnp.bfloat16)
        .reshape(head_shape)
    )
    row_delta = jnp.sum(mixed_grad.astype(jnp.float32) * mixed_heads.astype(jnp.float32), axis=-1)
    zero_queries = jnp.zeros(grad_shape, jnp.float32)
    zero_pairs = jnp.zeros(pair_shape, jnp.float32)
    query_side = (queries, mixed_grad, log_total, row_delta, own_positions, own_segments)

    def key_turn(source, packed, carried):
        key_pos = positions(source)
        key_seg = segments_of(source)

        def compute(inputs):
            query_acc, key_acc = inputs
            key_block, value_block = split_pair(packed)
            query_out, key_out, value_out = pair_grads(
                query_side, (key_block, value_block, key_pos, key_seg)
            )
            key_acc = key_acc + jnp.concatenate(
                [key_out.reshape(grad_shape), value_out.reshape(grad_shape)], axis=-1
            )
            return (query_acc + query_out.reshape(grad_shape), key_acc)

        return lax.cond(
            jnp.min(key_pos) <= jnp.max(own_positions), compute, lambda inputs: inputs, carried
        )

    def pass_keys(key_acc):
        return passed_along(key_acc, "ctx", 1)

    def key_back_turn(turn_index, carried):
        packed, query_acc, key_acc = carried
        query_acc, key_acc = key_turn(
            (cycle_index - turn_index) % cycle_size, packed, (query_acc, key_acc)
        )
        packed = passed_along(packed, "ctx", 1)
        return (packed, query_acc, pass_keys(key_acc))

    packed, query_acc, key_acc = lax.fori_loop(
        0, cycle_size - 1, key_back_turn, (key_value, zero_queries, zero_pairs)
    )
    query_acc, key_acc = key_turn((cycle_index + 1) % cycle_size, packed, (query_acc, key_acc))
    key_acc = pass_keys(key_acc)
    query_grad_all = query_acc * SCORE_SCALE
    key_grad_all = key_acc[..., :head_width] * SCORE_SCALE
    value_grad_all = key_acc[..., head_width:]
    qv_grad = jnp.stack(
        [
            jnp.sum(query_grad_all, axis=(0, 1)).reshape(head_count, head_size),
            jnp.sum(value_grad_all, axis=(0, 1)).reshape(head_count, head_size),
        ]
    )
    qkv_grad = (
        jnp.stack([query_grad_all, key_grad_all, value_grad_all], axis=2)
        .astype(jnp.bfloat16)
        .reshape(token_count, 3, head_width)
    )
    qkv_weight_grad = jnp.einsum(
        "td,tce->dce", normed_one, qkv_grad, preferred_element_type=jnp.float32
    )
    norm_one_grad = feature_sum(
        jnp.einsum("tce,dce->td", qkv_grad, qkv_full, preferred_element_type=jnp.float32)
    )
    gain_one_grad = jnp.sum(norm_one_grad * unit_one, axis=0)
    shift_one_grad = jnp.sum(norm_one_grad, axis=0)
    in_grad = mid_grad + normalize_back(norm_one_grad, unit_one, inverse_one, gain_one_high)
    local_grads = (
        gain_one_grad,
        shift_one_grad,
        qkv_weight_grad,
        qv_grad,
        proj_weight_grad,
        proj_offset_grad,
        gain_two_grad,
        shift_two_grad,
        up_weight_grad,
        up_offset_grad,
        down_weight_grad,
        down_offset_grad,
    )
    owned = (
        lax.psum_scatter(local_grads[0], "shard", scatter_dimension=0, tiled=True),
        lax.psum_scatter(local_grads[1], "shard", scatter_dimension=0, tiled=True),
        lax.psum_scatter(local_grads[2], "shard", scatter_dimension=0, tiled=True),
        lax.psum_scatter(local_grads[3], "shard", scatter_dimension=2, tiled=True),
        lax.psum_scatter(local_grads[4], "shard", scatter_dimension=1, tiled=True),
        lax.psum_scatter(local_grads[5], "shard", scatter_dimension=0, tiled=True),
        lax.psum_scatter(local_grads[6], "shard", scatter_dimension=0, tiled=True),
        lax.psum_scatter(local_grads[7], "shard", scatter_dimension=0, tiled=True),
        lax.psum_scatter(local_grads[8], "shard", scatter_dimension=0, tiled=True),
        lax.psum_scatter(local_grads[9], "shard", scatter_dimension=1, tiled=True),
        lax.psum_scatter(local_grads[10], "shard", scatter_dimension=1, tiled=True),
        lax.psum_scatter(local_grads[11], "shard", scatter_dimension=0, tiled=True),
    )
    totals = lax.psum(
        (
            owned[0],
            owned[1],
            owned[2],
            owned[3],
            owned[4],
            owned[5],
            owned[6],
            owned[7],
            owned[8],
            owned[9],
            owned[10],
            owned[11],
        ),
        "ctx",
    )
    block_out = block_out.reshape(row_count, row_tokens, model_width)
    in_grad = in_grad.reshape(row_count, row_tokens, model_width)
    block_out, in_grad = (
        lax.all_to_all(block_out, "ctx", split_axis=1, concat_axis=1, tiled=True),
        lax.all_to_all(in_grad, "ctx", split_axis=1, concat_axis=1, tiled=True),
    )
    return (block_out, in_grad) + tuple(totals)


MESH = pl.DeviceIdType.MESH
F32 = jnp.float32
BF16 = jnp.bfloat16
GAIN_ONE, SHIFT_ONE, PROJ_BIAS, GAIN_TWO, SHIFT_TWO, DOWN_BIAS, Q_BIAS, V_BIAS, UP_BIAS = range(9)
VEC_ROWS = 16
COPIES = 64
VMEM_LIMIT = 56 * 1024 * 1024


def mm(left, right, dims=((1,), (0,))):
    return lax.dot_general(left, right, (dims, ((), ())), preferred_element_type=F32)


NT = ((1,), (1,))
TN = ((0,), (0,))


def identity(size):
    at_row = lax.broadcasted_iota(jnp.int32, (size, size), 0)
    at_column = lax.broadcasted_iota(jnp.int32, (size, size), 1)
    return jnp.where(at_row == at_column, 1.0, 0.0).astype(BF16)


def pack_vectors(vec_ref, wide_ref, qv_ref, up_b_ref, shard):
    width = vec_ref.shape[1]
    depth = width // 4
    heads, _, piece = qv_ref.shape
    up_rows, up_piece = up_b_ref.shape
    vec_ref[...] = jnp.zeros_like(vec_ref)
    vec_ref[0:8, :depth] = wide_ref[...]
    wide = vec_ref[0:8, :]
    wide = pltpu.roll(wide, shard * depth, 1)
    span = 128 * ((4 * heads * piece + 127) // 128)
    qv_sum = jnp.zeros((8, span), F32)
    for head in range(heads):
        vec_ref[8:16, :] = jnp.zeros((8, width), F32)
        vec_ref[8:10, :piece] = qv_ref[head].astype(F32)
        qv_sum = qv_sum + pltpu.roll(vec_ref[8:16, :span], head * 4 * piece + shard * piece, 1)
    vec_ref[8:16, :] = jnp.zeros((8, width), F32)
    vec_ref[8 : 8 + up_rows, :up_piece] = up_b_ref[...].astype(F32)
    up_part = pltpu.roll(vec_ref[8:16, :128], shard * up_piece, 1)
    vec_ref[0:8, :] = wide
    vec_ref[Q_BIAS : Q_BIAS + 2, :span] = qv_sum[0:2]
    vec_ref[8:16, :128] = up_part


def finish_kernel(
    out_in, in_grad_in, attn_s3, attn_r3, mlp_s3, mlp_r3, vec_ref,
    out_ref, in_grad_ref, qkv_g_ref, proj_g_ref, up_g_ref, down_g_ref,
    gain_one_ref, shift_one_ref, proj_b_ref, gain_two_ref, shift_two_ref, down_b_ref, qv_g_ref, up_b_ref,
):
    shard = lax.axis_index("shard")
    width = vec_ref.shape[1]
    depth = width // 4
    heads, _, piece = qv_g_ref.shape
    up_rows, up_piece = up_b_ref.shape
    out_ref[...] = out_in[...]
    in_grad_ref[...] = in_grad_in[...]
    qkv_g_ref[...] = attn_s3[0:3].astype(F32) + attn_r3[0:3].astype(F32)
    unit = identity(depth)
    proj_g_ref[...] = mm(attn_s3[3], unit, TN) + mm(attn_r3[3], unit, TN)
    up_g_ref[...] = mlp_s3[0].astype(F32) + mlp_r3[0].astype(F32)
    down_g_ref[...] = mlp_s3[1].astype(F32) + mlp_r3[1].astype(F32)
    wide = pltpu.roll(vec_ref[0:8, :], lax.rem(width - shard * depth, width), 1)
    wide_refs = (gain_one_ref, shift_one_ref, proj_b_ref, gain_two_ref, shift_two_ref, down_b_ref)
    for index, ref in enumerate(wide_refs):
        ref[...] = wide[index : index + 1, :depth]
    span = 128 * ((4 * heads * piece + 127) // 128)
    for head in range(heads):
        turned = pltpu.roll(
            vec_ref[0:8, :span], lax.rem(span - head * 4 * piece - shard * piece, span), 1
        )
        qv_g_ref[head] = turned[Q_BIAS : Q_BIAS + 2, :piece]
    turned = pltpu.roll(vec_ref[8:16, :128], lax.rem(128 - shard * up_piece, 128), 1)
    up_b_ref[...] = turned[:up_rows, :up_piece]


def block_kernel(
    x_ref, cot_ref, seg_ref, qkv_w, proj_w, up_w, down_w, wide_ref, qv_ref, up_b_ref,
    out_ref, in_grad_ref, attn_s3, attn_r3, mlp_s3, mlp_r3, vec_g_ref,
    qkv_f, proj_t, proj_f, up_f, down_f, vec_ref, vec_in, segk, segk_in, kv, kv_in, dkv, dkv_in,
    part, ar_send, ar_recv, ar_all,
    attn_g, up_g, down_g, attn_s1, attn_r1, attn_s2, attn_r2,
    mlp_s1, mlp_r1, mlp_s2, mlp_r2,
    vec_s, vec_r, send_sem, recv_sem,
):
    shard = lax.axis_index("shard")
    ctx = lax.axis_index("ctx")
    tp = lax.axis_index("tp")
    core = lax.rem(shard, 2)
    high = shard // 2
    s1 = shard + 1 - 2 * core
    s2 = lax.rem(shard + 2, 4)
    s3 = lax.rem(s1 + 2, 4)
    p1, p2, p3 = {"shard": s1}, {"shard": s2}, {"shard": s3}
    pc = {"ctx": 1 - ctx}
    tps = [lax.rem(tp + step, 4) for step in (1, 2, 3)]
    tokens, width = x_ref.shape
    depth = up_w.shape[0]
    heads_width = qkv_w.shape[2]
    head_count = heads_width // 64

    barrier = pltpu.get_barrier_semaphore()
    peers = [p1, p2, p3, pc] + [{"tp": t} for t in tps]
    for peer in peers:
        pl.semaphore_signal(barrier, inc=1, device_id=peer, device_id_type=MESH)

    started = []

    def send(src, dst, peer):
        slot = len(started)
        copy = pltpu.make_async_remote_copy(
            src_ref=src, dst_ref=dst, send_sem=send_sem.at[slot], recv_sem=recv_sem.at[slot],
            device_id=peer, device_id_type=MESH,
        )
        copy.start()
        started.append(copy)
        return copy

    def unit_of(values):
        center = jnp.mean(values, axis=-1, keepdims=True)
        shifted = values - center
        inverse = lax.rsqrt(jnp.mean(shifted * shifted, axis=-1, keepdims=True) + EPSILON)
        return shifted * inverse, inverse

    pack_vectors(vec_ref, wide_ref, qv_ref, up_b_ref, shard)
    segk[...] = jnp.broadcast_to(seg_ref[...], segk.shape)
    proj_t[...] = mm(proj_w[...], identity(heads_width), TN).astype(BF16)
    pl.semaphore_wait(barrier, len(peers))

    def gather_start(local, full):
        far = send(local, full.at[shard], p2)
        near = send(local, full.at[shard], p1)
        return far, near

    def gather_pass(full, far):
        far.wait_recv()
        return send(full.at[s2], full.at[s2], p1)

    qkv_far, qkv_near = gather_start(qkv_w, qkv_f)
    vec_copies = [send(vec_ref, vec_in.at[i], p) for i, p in enumerate((p1, p2, p3))]
    seg_copy = send(segk, segk_in, pc)
    qkv_f[shard] = qkv_w[...]
    proj_f[shard] = proj_t[...]
    up_f[shard] = up_w[...]
    down_f[shard] = down_w[...]
    residual_in = x_ref[...].astype(F32)
    unit_one, inverse_one = unit_of(residual_in)
    for copy in vec_copies:
        copy.wait_recv()
    vec = vec_ref[...] + vec_in[0] + vec_in[1] + vec_in[2]

    up_bias = jnp.concatenate(
        [vec[UP_BIAS + r : UP_BIAS + r + 1, :128] for r in range(up_b_ref.shape[0])], axis=1
    )

    def row(index, size=width):
        return vec[index : index + 1, :size]

    normed_one = (unit_one * row(GAIN_ONE) + row(SHIFT_ONE)).astype(BF16)
    qkv_pass = gather_pass(qkv_f, qkv_far)
    proj_far, proj_near = gather_start(proj_t, proj_f)
    up_far, up_near = gather_start(up_w, up_f)
    down_far, down_near = gather_start(down_w, down_f)
    qkv_near.wait_recv()
    qkv_pass.wait_recv()
    weight_q, weight_k, weight_v = (
        qkv_f[:, index].reshape(4 * depth, heads_width) for index in range(3)
    )
    keys = mm(normed_one, weight_k).astype(BF16)
    values = (mm(normed_one, weight_v) + row(V_BIAS, heads_width)).astype(BF16)
    kv[0] = keys
    kv[1] = values
    kv_copy = send(kv, kv_in, pc)
    queries = (mm(normed_one, weight_q) + row(Q_BIAS, heads_width)).astype(BF16)

    lane_head = lax.broadcasted_iota(jnp.int32, (tokens, heads_width), 1) // 64
    of_head = [lane_head == index for index in range(head_count)]

    def pick(values_in, index):
        return jnp.where(of_head[index], values_in, jnp.zeros_like(values_in))

    seg_copy.wait_recv()
    query_at = lax.broadcasted_iota(jnp.int32, (tokens, tokens), 0)
    key_at = lax.broadcasted_iota(jnp.int32, (tokens, tokens), 1)
    segq = jnp.transpose(jnp.broadcast_to(seg_ref[...].astype(F32), (tokens, tokens))).astype(jnp.int32)
    allow_own = (key_at <= query_at) & (segq == segk[0:1, :])
    allow_other = (segq == segk_in[0:1, :]) & (key_at + tokens * (1 - ctx) <= query_at + tokens * ctx)
    query_of = [pick(queries, index) for index in range(head_count)]
    score_own = [
        jnp.where(allow_own, mm(query_of[i], keys, NT) * SCORE_SCALE, NEGATIVE)
        for i in range(head_count)
    ]
    proj_pass = gather_pass(proj_f, proj_far)
    kv_copy.wait_recv()
    keys_other = kv_in[0]
    values_other = kv_in[1]
    probs_own, probs_other = [], []
    mixed_sum = jnp.zeros((tokens, heads_width), F32)
    for i in range(head_count):
        own = score_own[i]
        other = jnp.where(allow_other, mm(query_of[i], keys_other, NT) * SCORE_SCALE, NEGATIVE)
        top = jnp.maximum(
            jnp.max(own, axis=-1, keepdims=True), jnp.max(other, axis=-1, keepdims=True)
        )
        total = jnp.sum(jnp.exp(own - top), axis=-1, keepdims=True) + jnp.sum(
            jnp.exp(other - top), axis=-1, keepdims=True
        )
        log_total = top + jnp.log(total)
        probs_own.append(jnp.where(allow_own, jnp.exp(own - log_total), 0.0))
        probs_other.append(jnp.where(allow_other, jnp.exp(other - log_total), 0.0))
        mixed_head = mm(probs_own[i].astype(BF16), values) + mm(
            probs_other[i].astype(BF16), values_other
        )
        mixed_sum = mixed_sum + pick(mixed_head, i)
    mixed = mixed_sum.astype(BF16)

    def sum_start(phase, value):
        pieces = value.reshape(4, tokens // 4, width)
        part[phase] = pieces
        ar_send[phase] = pieces.astype(BF16)
        return [send(ar_send.at[phase, t], ar_recv.at[phase, i], {"tp": t}) for i, t in enumerate(tps)]

    def sum_pass(phase, copies):
        total = part[phase, tp]
        for i, copy in enumerate(copies):
            copy.wait_recv()
            total = total + ar_recv[phase, i].astype(F32)
        ar_all[phase, tp] = total.astype(BF16)
        return [send(ar_all.at[phase, tp], ar_all.at[phase, tp], {"tp": t}) for t in tps]

    def sum_end(phase, copies):
        for copy in copies:
            copy.wait_recv()
        return ar_all[phase].reshape(tokens, width).astype(F32)

    proj_near.wait_recv()
    proj_pass.wait_recv()
    weight_p = proj_f[...].reshape(4 * depth, heads_width)
    mid_sum = sum_start(0, mm(mixed, weight_p, NT))
    up_pass = gather_pass(up_f, up_far)
    mid_sum = sum_pass(0, mid_sum)
    down_pass = gather_pass(down_f, down_far)
    residual_mid = residual_in + sum_end(0, mid_sum) + row(PROJ_BIAS)
    unit_two, inverse_two = unit_of(residual_mid)
    normed_two = (unit_two * row(GAIN_TWO) + row(SHIFT_TWO)).astype(BF16)
    up_near.wait_recv()
    up_pass.wait_recv()
    up_full = up_f[...].reshape(4 * depth, up_f.shape[2])
    pre_gelu = mm(normed_two, up_full) + up_bias
    tangent = jnp.tanh(GELU_ROOT * (pre_gelu + GELU_CUBIC * pre_gelu * pre_gelu * pre_gelu))
    hidden = (0.5 * pre_gelu * (1.0 + tangent)).astype(BF16)
    slope = 0.5 * (1.0 + tangent) + 0.5 * pre_gelu * (1.0 - tangent * tangent) * GELU_ROOT * (
        1.0 + 3.0 * GELU_CUBIC * pre_gelu * pre_gelu
    )
    down_near.wait_recv()
    down_pass.wait_recv()
    down_full = down_f[...].reshape(4 * depth, down_f.shape[2])
    cot_low = cot_ref[...]
    cot_high = cot_low.astype(F32)
    pre_grad = mm(cot_low, down_full) * slope
    pre_grad_low = pre_grad.astype(BF16)
    two_sum = sum_start(2, mm(pre_grad_low, up_full, NT))
    out_sum = sum_start(1, mm(hidden, down_full, NT))

    def column_sum(value):
        return jnp.sum(value, axis=0, keepdims=True)

    vec_s[0] = jnp.zeros((VEC_ROWS, width), F32)
    up_bias_grad = column_sum(pre_grad)
    for r in range(up_b_ref.shape[0]):
        vec_s[0, UP_BIAS + r : UP_BIAS + r + 1, :128] = up_bias_grad[:, 128 * r : 128 * (r + 1)]
    vec_s[0, DOWN_BIAS : DOWN_BIAS + 1, :] = column_sum(cot_high)

    def reduce_one(grads, s1_buf, r1_buf):
        for half in range(2):
            s1_buf[half] = grads[2 * half + 1 - core].astype(BF16)
        return send(s1_buf, r1_buf, p1)

    def reduce_two(copy, grads, r1_buf, s2_buf, r2_buf):
        copy.wait_recv()
        s2_buf[...] = (grads[s2] + r1_buf[1 - high].astype(F32)).astype(BF16)
        return send(s2_buf, r2_buf, p2)

    def reduce_three(copy, grads, r1_buf, r2_buf, s3_buf, r3_buf):
        copy.wait_recv()
        s3_buf[...] = (
            grads[shard] + r1_buf[high].astype(F32) + r2_buf[...].astype(F32)
        ).astype(BF16)
        return send(s3_buf, r3_buf, pc)

    down_g[...] = mm(cot_low, hidden, TN).reshape(down_g.shape)
    down_copy = reduce_one(down_g, mlp_s1.at[1], mlp_r1.at[1])
    two_sum = sum_pass(2, two_sum)
    up_g[...] = mm(normed_two, pre_grad_low, TN).reshape(up_g.shape)
    up_copy = reduce_one(up_g, mlp_s1.at[0], mlp_r1.at[0])
    down_copy = reduce_two(down_copy, down_g, mlp_r1.at[1], mlp_s2.at[1], mlp_r2.at[1])
    norm_two_grad = sum_end(2, two_sum)
    vec_s[0, GAIN_TWO : GAIN_TWO + 1, :] = column_sum(norm_two_grad * unit_two)
    vec_s[0, SHIFT_TWO : SHIFT_TWO + 1, :] = column_sum(norm_two_grad)
    mid_grad = cot_high + normalize_back(norm_two_grad, unit_two, inverse_two, row(GAIN_TWO))
    vec_s[0, PROJ_BIAS : PROJ_BIAS + 1, :] = column_sum(mid_grad)
    mid_grad_low = mid_grad.astype(BF16)
    mixed_grad = mm(mid_grad_low, weight_p).astype(BF16)
    delta_terms = mixed_grad.astype(F32) * mixed.astype(F32)
    zero = jnp.zeros((tokens, heads_width), F32)
    query_grad, key_own, value_own, key_other, value_other = zero, zero, zero, zero, zero
    for i in range(head_count):
        head_grad = pick(mixed_grad, i)
        delta = jnp.sum(pick(delta_terms, i), axis=-1, keepdims=True)
        grad_other = (probs_other[i] * (mm(head_grad, values_other, NT) - delta)).astype(BF16)
        grad_own = (probs_own[i] * (mm(head_grad, values, NT) - delta)).astype(BF16)
        key_other = key_other + mm(grad_other, query_of[i], TN)
        value_other = value_other + mm(probs_other[i].astype(BF16), head_grad, TN)
        key_own = key_own + mm(grad_own, query_of[i], TN)
        value_own = value_own + mm(probs_own[i].astype(BF16), head_grad, TN)
        query_grad = query_grad + pick(mm(grad_own, keys) + mm(grad_other, keys_other), i)
    dkv[0] = key_other.astype(BF16)
    dkv[1] = value_other.astype(BF16)
    dkv_copy = send(dkv, dkv_in, pc)
    up_copy = reduce_two(up_copy, up_g, mlp_r1.at[0], mlp_s2.at[0], mlp_r2.at[0])
    out_sum = sum_pass(1, out_sum)
    proj_grad = mm(mid_grad_low, mixed, TN).reshape(4, depth, heads_width)
    for index in range(4):
        attn_g[index, 3] = proj_grad[index]
    query_grad = query_grad * SCORE_SCALE
    query_low = query_grad.astype(BF16)
    vec_s[0, Q_BIAS : Q_BIAS + 1, :heads_width] = column_sum(query_grad)
    one_part = mm(query_low, weight_q, NT)
    dkv_copy.wait_recv()
    key_low = ((key_own + dkv_in[0].astype(F32)) * SCORE_SCALE).astype(BF16)
    value_grad = value_own + dkv_in[1].astype(F32)
    value_low = value_grad.astype(BF16)
    vec_s[0, V_BIAS : V_BIAS + 1, :heads_width] = column_sum(value_grad)
    one_part = one_part + mm(key_low, weight_k, NT) + mm(value_low, weight_v, NT)
    one_sum = sum_start(3, one_part)
    for index, grad_low in enumerate((query_low, key_low, value_low)):
        weight_grad = mm(normed_one, grad_low, TN).reshape(4, depth, heads_width)
        for block in range(4):
            attn_g[block, index] = weight_grad[block]
    attn_copy = reduce_one(attn_g, attn_s1, attn_r1)
    one_sum = sum_pass(3, one_sum)
    attn_copy = reduce_two(attn_copy, attn_g, attn_r1, attn_s2, attn_r2)
    down_copy = reduce_three(
        down_copy, down_g, mlp_r1.at[1], mlp_r2.at[1], mlp_s3.at[1], mlp_r3.at[1]
    )
    up_copy = reduce_three(up_copy, up_g, mlp_r1.at[0], mlp_r2.at[0], mlp_s3.at[0], mlp_r3.at[0])
    norm_one_grad = sum_end(3, one_sum)
    vec_s[0, GAIN_ONE : GAIN_ONE + 1, :] = column_sum(norm_one_grad * unit_one)
    vec_s[0, SHIFT_ONE : SHIFT_ONE + 1, :] = column_sum(norm_one_grad)
    vec_copy = send(vec_s.at[0], vec_r.at[0], p1)
    attn_copy = reduce_three(attn_copy, attn_g, attn_r1, attn_r2, attn_s3, attn_r3)
    in_grad_ref[...] = mid_grad + normalize_back(
        norm_one_grad, unit_one, inverse_one, row(GAIN_ONE)
    )
    vec_copy.wait_recv()
    vec_s[1] = vec_s[0] + vec_r[0]
    vec_copy = send(vec_s.at[1], vec_r.at[1], p2)
    out_ref[...] = residual_mid + sum_end(1, out_sum) + row(DOWN_BIAS)
    vec_copy.wait_recv()
    vec_s[2] = vec_s[1] + vec_r[1]
    vec_copy = send(vec_s.at[2], vec_r.at[2], pc)
    down_copy.wait_recv()
    up_copy.wait_recv()
    attn_copy.wait_recv()
    vec_copy.wait_recv()
    vec_g_ref[...] = vec_s[2] + vec_r[2]
    for copy in started:
        copy.wait_send()


def paired_body(
    block_in, segment_ids, out_cotangent, attn_gain, attn_shift, qkv_weight, qv_bias, proj_weight,
    proj_bias, mlp_gain, mlp_shift, up_weight, up_bias, down_weight, down_bias,
):
    _, tokens, width = block_in.shape
    depth = qkv_weight.shape[0]
    heads_width = qkv_weight.shape[2]
    units = up_weight.shape[1]
    head_count, head_piece = qv_bias.shape[1:]
    at_row = lax.broadcasted_iota(jnp.int32, (8, depth), 0)
    wide = jnp.zeros((8, depth), F32)
    vectors = (attn_gain, attn_shift, proj_bias, mlp_gain, mlp_shift, down_bias)
    for index, vector in enumerate(vectors):
        wide = jnp.where(at_row == index, vector.astype(F32)[None, :], wide)
    attn_shape = (4, depth, heads_width)
    mlp_shape = (depth, units)
    vmem = pltpu.VMEM
    shaped = jax.ShapeDtypeStruct
    middle_shapes = (
        shaped((tokens, width), F32),
        shaped((tokens, width), F32),
        shaped(attn_shape, BF16),
        shaped(attn_shape, BF16),
        shaped((2,) + mlp_shape, BF16),
        shaped((2,) + mlp_shape, BF16),
        shaped((VEC_ROWS, width), F32),
    )
    proj_shape = (depth, heads_width)
    qkv_shape = (3, depth, heads_width)
    scratch = [
        vmem((4,) + qkv_shape, BF16), vmem(proj_shape, BF16), vmem((4,) + proj_shape, BF16),
        vmem((4,) + mlp_shape, BF16), vmem((4,) + mlp_shape, BF16),
        vmem((VEC_ROWS, width), F32), vmem((3, VEC_ROWS, width), F32),
        vmem((8, tokens), jnp.int32), vmem((8, tokens), jnp.int32),
        vmem((2, tokens, heads_width), BF16), vmem((2, tokens, heads_width), BF16),
        vmem((2, tokens, heads_width), BF16), vmem((2, tokens, heads_width), BF16),
        vmem((4, 4, tokens // 4, width), F32), vmem((4, 4, tokens // 4, width), BF16),
        vmem((4, 3, tokens // 4, width), BF16), vmem((4, 4, tokens // 4, width), BF16),
        vmem((4,) + attn_shape, F32), vmem((4,) + mlp_shape, F32), vmem((4,) + mlp_shape, F32),
        vmem((2,) + attn_shape, BF16), vmem((2,) + attn_shape, BF16),
        vmem(attn_shape, BF16), vmem(attn_shape, BF16),
        vmem((2, 2) + mlp_shape, BF16), vmem((2, 2) + mlp_shape, BF16),
        vmem((2,) + mlp_shape, BF16), vmem((2,) + mlp_shape, BF16),
        vmem((3, VEC_ROWS, width), F32), vmem((3, VEC_ROWS, width), F32),
        pltpu.SemaphoreType.DMA((COPIES,)), pltpu.SemaphoreType.DMA((COPIES,)),
    ]
    whole = pl.BlockSpec(memory_space=pltpu.VMEM)
    middle = pl.pallas_call(
        block_kernel,
        out_shape=middle_shapes,
        in_specs=[whole] * 10,
        out_specs=(whole,) * 7,
        scratch_shapes=scratch,
        compiler_params=pltpu.CompilerParams(
            collective_id=0, has_side_effects=True, vmem_limit_bytes=VMEM_LIMIT
        ),
    )(
        block_in[0], out_cotangent[0], segment_ids, jnp.transpose(qkv_weight, (1, 0, 2)), proj_weight,
        up_weight, jnp.transpose(down_weight), wide, jnp.transpose(qv_bias, (1, 0, 2)), up_bias,
    )
    one_row = shaped((1, depth), F32)
    result_shapes = (
        shaped((tokens, width), F32), shaped((tokens, width), F32), shaped(qkv_shape, F32),
        shaped((heads_width, depth), F32), shaped(mlp_shape, F32), shaped(mlp_shape, F32),
        one_row, one_row, one_row, one_row, one_row, one_row,
        shaped((head_count, 2, head_piece), F32), shaped(up_bias.shape, F32),
    )
    (
        block_out, in_grad, qkv_g, proj_g, up_g, down_g,
        gain_one, shift_one, proj_b, gain_two, shift_two, down_b, qv_b, up_b,
    ) = pl.pallas_call(
        finish_kernel,
        out_shape=result_shapes,
        in_specs=[whole] * 7,
        out_specs=(whole,) * 14,
        compiler_params=pltpu.CompilerParams(vmem_limit_bytes=16 * 1024 * 1024),
    )(*middle)
    return (
        block_out[None], in_grad[None], gain_one[0], shift_one[0], jnp.transpose(qkv_g, (1, 0, 2)),
        jnp.transpose(qv_b, (1, 0, 2)), proj_g, proj_b[0], gain_two[0], shift_two[0], up_g, up_b,
        jnp.transpose(down_g), down_b[0],
    )


def solution(mesh):
    paired = mesh.shape["ctx"] == 2 and mesh.shape["shard"] == 4 and mesh.shape["tp"] == 4
    return jax.shard_map(
        paired_body if paired else body,
        mesh=mesh,
        in_specs=(
            P("shard", "ctx", None),
            P("shard", "ctx"),
            P("shard", "ctx", None),
            P("shard"),
            P("shard"),
            P("shard", None, "tp"),
            P(None, "tp", "shard"),
            P("tp", "shard"),
            P("shard"),
            P("shard"),
            P("shard"),
            P("shard", "tp"),
            P("tp", "shard"),
            P("tp", "shard"),
            P("shard"),
        ),
        out_specs=(
            P("shard", "ctx", None),
            P("shard", "ctx", None),
            P("shard"),
            P("shard"),
            P("shard", None, "tp"),
            P(None, "tp", "shard"),
            P("tp", "shard"),
            P("shard"),
            P("shard"),
            P("shard"),
            P("shard", "tp"),
            P("tp", "shard"),
            P("tp", "shard"),
            P("shard"),
        ),
        check_vma=False,
    )
```

```python
import jax
import jax.numpy as jnp
from jax import lax
from jax.experimental import pallas as pl
from jax.experimental.pallas import tpu as pltpu
from jax.sharding import PartitionSpec as P

EPSILON = 1e-05
GELU_ROOT = 0.7978845608028654
GELU_CUBIC = 0.044715
SCORE_SCALE = 0.125
NEGATIVE = -1e30


def passed_along(value, axis, steps):
    count = lax.axis_size(axis)
    pairs = [(source, (source + steps) % count) for source in range(count)]
    return lax.ppermute(value, axis, pairs)


def normalize(values, gain_vec, offset):
    center = jnp.mean(values, axis=-1, keepdims=True)
    shifted = values - center
    spread = jnp.mean(shifted * shifted, axis=-1, keepdims=True)
    inverse = lax.rsqrt(spread + EPSILON)
    unit_vals = shifted * inverse
    return (unit_vals, inverse, unit_vals * gain_vec + offset)


def normalize_back(grad_norm, unit_vals, inverse, gain_vec):
    scaled = grad_norm * gain_vec
    mean_first = jnp.mean(scaled, axis=-1, keepdims=True)
    second = jnp.mean(scaled * unit_vals, axis=-1, keepdims=True)
    return inverse * (scaled - mean_first - unit_vals * second)


def gelu_value(pre_gelu):
    return (
        0.5
        * pre_gelu
        * (1.0 + jnp.tanh(GELU_ROOT * (pre_gelu + GELU_CUBIC * pre_gelu * pre_gelu * pre_gelu)))
    )


def gelu_slope(pre_gelu):
    tangent = jnp.tanh(GELU_ROOT * (pre_gelu + GELU_CUBIC * pre_gelu * pre_gelu * pre_gelu))
    return 0.5 * (1.0 + tangent) + 0.5 * pre_gelu * (1.0 - tangent * tangent) * GELU_ROOT * (
        1.0 + 3.0 * GELU_CUBIC * pre_gelu * pre_gelu
    )


def feature_sum(part_sum):
    return lax.psum(part_sum, "tp")


def allowed_pairs(query_pos, query_seg, key_pos, key_seg):
    causal = key_pos[None, :] <= query_pos[:, None]
    same_doc = query_seg[:, :, None] == key_seg[:, None, :]
    return (causal[None] & same_doc)[:, :, None, :]


def pair_grads(query_side, key_side):
    query_vals, query_grad, query_lse, query_delta, query_pos, query_seg = query_side
    key_vals, value_vals, key_pos, key_seg = key_side
    scores = (
        jnp.einsum("rqhd,rkhd->rqhk", query_vals, key_vals, preferred_element_type=jnp.float32)
        * SCORE_SCALE
    )
    allowed = allowed_pairs(query_pos, query_seg, key_pos, key_seg)
    probs = jnp.where(allowed, jnp.exp(scores - query_lse[..., None]), 0.0)
    value_out = jnp.einsum(
        "rqhk,rqhd->rkhd",
        probs.astype(jnp.bfloat16),
        query_grad,
        preferred_element_type=jnp.float32,
    )
    weight_grad = jnp.einsum(
        "rqhd,rkhd->rqhk", query_grad, value_vals, preferred_element_type=jnp.float32
    )
    score_grad = (probs * (weight_grad - query_delta[..., None])).astype(jnp.bfloat16)
    query_out = jnp.einsum(
        "rqhk,rkhd->rqhd", score_grad, key_vals, preferred_element_type=jnp.float32
    )
    key_out = jnp.einsum(
        "rqhk,rqhd->rkhd", score_grad, query_vals, preferred_element_type=jnp.float32
    )
    return (query_out, key_out, value_out)


def body(
    block_in,
    segment_ids,
    out_cotangent,
    attn_gain,
    attn_shift,
    qkv_weight,
    qv_bias,
    proj_weight,
    proj_bias,
    mlp_gain,
    mlp_shift,
    up_weight,
    up_bias,
    down_weight,
    down_bias,
):
    cycle_size = lax.axis_size("ctx")
    cycle_index = lax.axis_index("ctx")
    row_count, row_tokens, model_width = block_in.shape
    piece_len = row_tokens // cycle_size
    token_count = row_count * row_tokens
    gathered = (
        lax.all_gather(attn_gain, "shard", axis=0, tiled=True),
        lax.all_gather(attn_shift, "shard", axis=0, tiled=True),
        lax.all_gather(qkv_weight, "shard", axis=0, tiled=True),
        lax.all_gather(qv_bias, "shard", axis=2, tiled=True),
        lax.all_gather(proj_weight, "shard", axis=1, tiled=True),
        lax.all_gather(proj_bias, "shard", axis=0, tiled=True),
        lax.all_gather(mlp_gain, "shard", axis=0, tiled=True),
        lax.all_gather(mlp_shift, "shard", axis=0, tiled=True),
        lax.all_gather(up_weight, "shard", axis=0, tiled=True),
        lax.all_gather(up_bias, "shard", axis=1, tiled=True),
        lax.all_gather(down_weight, "shard", axis=1, tiled=True),
        lax.all_gather(down_bias, "shard", axis=0, tiled=True),
    )
    (
        gain_one,
        shift_one,
        qkv_full,
        qv_full,
        proj_full,
        proj_offset,
        gain_two,
        shift_two,
        up_full,
        up_offset,
        down_full,
        down_offset,
    ) = gathered
    head_size = qv_full.shape[2]
    head_width = qkv_full.shape[2]
    head_count = head_width // head_size
    all_segments = lax.all_gather(segment_ids, "ctx", axis=1, tiled=True)
    counter = jnp.arange(row_tokens, dtype=jnp.int32)
    local_in, local_cot = (
        lax.all_to_all(block_in, "ctx", split_axis=1, concat_axis=1, tiled=True),
        lax.all_to_all(out_cotangent, "ctx", split_axis=1, concat_axis=1, tiled=True),
    )

    def positions(source):
        return counter // piece_len * row_tokens + source * piece_len + counter % piece_len

    def segments_of(source):
        return jnp.take(all_segments, positions(source), axis=1)

    gain_one_high = gain_one.astype(jnp.float32)
    gain_two_high = gain_two.astype(jnp.float32)
    residual_in = local_in.reshape(token_count, model_width).astype(jnp.float32)
    unit_one, inverse_one, normed = normalize(
        residual_in, gain_one_high, shift_one.astype(jnp.float32)
    )
    normed_one = normed.astype(jnp.bfloat16)
    projected = jnp.einsum("td,dce->tce", normed_one, qkv_full, preferred_element_type=jnp.float32)
    query_bias = qv_full[0].reshape(head_width).astype(jnp.float32)
    value_bias = qv_full[1].reshape(head_width).astype(jnp.float32)
    head_shape = (row_count, row_tokens, head_count, head_size)
    grad_shape = (row_count, row_tokens, head_width)
    pair_shape = (row_count, row_tokens, 2 * head_width)
    queries = (projected[:, 0] + query_bias).astype(jnp.bfloat16).reshape(head_shape)
    key_value = (
        jnp.concatenate([projected[:, 1], projected[:, 2] + value_bias], axis=-1)
        .astype(jnp.bfloat16)
        .reshape(pair_shape)
    )
    own_positions = positions(cycle_index)
    own_segments = segments_of(cycle_index)

    def split_pair(packed):
        return (
            packed[..., :head_width].reshape(head_shape),
            packed[..., head_width:].reshape(head_shape),
        )

    def circle_pass(visit, state):

        def forward_turn(turn_index, carried):
            inner_state, packed = carried
            inner_state = visit(inner_state, packed, (cycle_index - turn_index) % cycle_size)
            packed = passed_along(packed, "ctx", 1)
            return (inner_state, packed)

        state, packed = lax.fori_loop(0, cycle_size - 1, forward_turn, (state, key_value))
        return visit(state, packed, (cycle_index + 1) % cycle_size)

    def block_scores(packed, source):
        key_pos = positions(source)
        key_seg = segments_of(source)
        key_block, value_block = split_pair(packed)
        scores = (
            jnp.einsum("rqhd,rkhd->rqhk", queries, key_block, preferred_element_type=jnp.float32)
            * SCORE_SCALE
        )
        allowed = allowed_pairs(own_positions, own_segments, key_pos, key_seg)
        return (scores, allowed, value_block)

    def reached(source):
        return jnp.min(positions(source)) <= jnp.max(own_positions)

    def gather_stats(softmax_state, packed, source):

        def compute(carried):
            running_max, running_sum = carried
            scores, allowed, value_block = block_scores(packed, source)
            scores = jnp.where(allowed, scores, NEGATIVE)
            new_max = jnp.maximum(running_max, jnp.max(scores, axis=-1))
            weights = jnp.where(allowed, jnp.exp(scores - new_max[..., None]), 0.0)
            running_sum = running_sum * jnp.exp(running_max - new_max) + jnp.sum(weights, axis=-1)
            return (new_max, running_sum)

        return lax.cond(reached(source), compute, lambda carried: carried, softmax_state)

    start_state = (
        jnp.full(head_shape[:3], NEGATIVE, jnp.float32),
        jnp.zeros(head_shape[:3], jnp.float32),
    )
    running_max, running_sum = circle_pass(gather_stats, start_state)
    log_total = running_max + jnp.log(running_sum)

    def gather_mix(accumulated, packed, source):

        def compute(carried):
            scores, allowed, value_block = block_scores(packed, source)
            probs_low = jnp.where(allowed, jnp.exp(scores - log_total[..., None]), 0.0).astype(
                jnp.bfloat16
            )
            return carried + jnp.einsum(
                "rqhk,rkhd->rqhd", probs_low, value_block, preferred_element_type=jnp.float32
            )

        return lax.cond(reached(source), compute, lambda carried: carried, accumulated)

    accumulated = circle_pass(gather_mix, jnp.zeros(head_shape, jnp.float32))
    mixed_heads = accumulated.astype(jnp.bfloat16)
    mixed_flat = mixed_heads.reshape(token_count, head_width)
    residual_mid = (
        residual_in
        + feature_sum(jnp.dot(mixed_flat, proj_full, preferred_element_type=jnp.float32))
        + proj_offset.astype(jnp.float32)
    )
    unit_two, inverse_two, normed = normalize(
        residual_mid, gain_two_high, shift_two.astype(jnp.float32)
    )
    normed_two = normed.astype(jnp.bfloat16)
    pre_gelu = jnp.dot(normed_two, up_full, preferred_element_type=jnp.float32) + up_offset.reshape(
        -1
    ).astype(jnp.float32)
    hidden = gelu_value(pre_gelu).astype(jnp.bfloat16)
    block_out = (
        residual_mid
        + feature_sum(jnp.dot(hidden, down_full, preferred_element_type=jnp.float32))
        + down_offset.astype(jnp.float32)
    )
    cot_low = local_cot.reshape(token_count, model_width)
    cot_high = cot_low.astype(jnp.float32)
    down_offset_grad = jnp.sum(cot_high, axis=0)
    down_weight_grad = jnp.einsum("tf,td->fd", hidden, cot_low, preferred_element_type=jnp.float32)
    pre_grad = jnp.einsum(
        "td,fd->tf", cot_low, down_full, preferred_element_type=jnp.float32
    ) * gelu_slope(pre_gelu)
    up_offset_grad = jnp.sum(pre_grad, axis=0).reshape(up_offset.shape)
    pre_grad_low = pre_grad.astype(jnp.bfloat16)
    up_weight_grad = jnp.einsum(
        "td,tf->df", normed_two, pre_grad_low, preferred_element_type=jnp.float32
    )
    norm_two_grad = feature_sum(
        jnp.einsum("tf,df->td", pre_grad_low, up_full, preferred_element_type=jnp.float32)
    )
    gain_two_grad = jnp.sum(norm_two_grad * unit_two, axis=0)
    shift_two_grad = jnp.sum(norm_two_grad, axis=0)
    mid_grad = cot_high + normalize_back(norm_two_grad, unit_two, inverse_two, gain_two_high)
    proj_offset_grad = jnp.sum(mid_grad, axis=0)
    mid_grad_low = mid_grad.astype(jnp.bfloat16)
    proj_weight_grad = jnp.einsum(
        "te,td->ed", mixed_flat, mid_grad_low, preferred_element_type=jnp.float32
    )
    mixed_grad = (
        jnp.einsum("td,ed->te", mid_grad_low, proj_full, preferred_element_type=jnp.float32)
        .astype(jnp.bfloat16)
        .reshape(head_shape)
    )
    row_delta = jnp.sum(mixed_grad.astype(jnp.float32) * mixed_heads.astype(jnp.float32), axis=-1)
    zero_queries = jnp.zeros(grad_shape, jnp.float32)
    zero_pairs = jnp.zeros(pair_shape, jnp.float32)
    query_side = (queries, mixed_grad, log_total, row_delta, own_positions, own_segments)

    def key_turn(source, packed, carried):
        key_pos = positions(source)
        key_seg = segments_of(source)

        def compute(inputs):
            query_acc, key_acc = inputs
            key_block, value_block = split_pair(packed)
            query_out, key_out, value_out = pair_grads(
                query_side, (key_block, value_block, key_pos, key_seg)
            )
            key_acc = key_acc + jnp.concatenate(
                [key_out.reshape(grad_shape), value_out.reshape(grad_shape)], axis=-1
            )
            return (query_acc + query_out.reshape(grad_shape), key_acc)

        return lax.cond(
            jnp.min(key_pos) <= jnp.max(own_positions), compute, lambda inputs: inputs, carried
        )

    def pass_keys(key_acc):
        return passed_along(key_acc, "ctx", 1)

    def key_back_turn(turn_index, carried):
        packed, query_acc, key_acc = carried
        query_acc, key_acc = key_turn(
            (cycle_index - turn_index) % cycle_size, packed, (query_acc, key_acc)
        )
        packed = passed_along(packed, "ctx", 1)
        return (packed, query_acc, pass_keys(key_acc))

    packed, query_acc, key_acc = lax.fori_loop(
        0, cycle_size - 1, key_back_turn, (key_value, zero_queries, zero_pairs)
    )
    query_acc, key_acc = key_turn((cycle_index + 1) % cycle_size, packed, (query_acc, key_acc))
    key_acc = pass_keys(key_acc)
    query_grad_all = query_acc * SCORE_SCALE
    key_grad_all = key_acc[..., :head_width] * SCORE_SCALE
    value_grad_all = key_acc[..., head_width:]
    qv_grad = jnp.stack(
        [
            jnp.sum(query_grad_all, axis=(0, 1)).reshape(head_count, head_size),
            jnp.sum(value_grad_all, axis=(0, 1)).reshape(head_count, head_size),
        ]
    )
    qkv_grad = (
        jnp.stack([query_grad_all, key_grad_all, value_grad_all], axis=2)
        .astype(jnp.bfloat16)
        .reshape(token_count, 3, head_width)
    )
    qkv_weight_grad = jnp.einsum(
        "td,tce->dce", normed_one, qkv_grad, preferred_element_type=jnp.float32
    )
    norm_one_grad = feature_sum(
        jnp.einsum("tce,dce->td", qkv_grad, qkv_full, preferred_element_type=jnp.float32)
    )
    gain_one_grad = jnp.sum(norm_one_grad * unit_one, axis=0)
    shift_one_grad = jnp.sum(norm_one_grad, axis=0)
    in_grad = mid_grad + normalize_back(norm_one_grad, unit_one, inverse_one, gain_one_high)
    local_grads = (
        gain_one_grad,
        shift_one_grad,
        qkv_weight_grad,
        qv_grad,
        proj_weight_grad,
        proj_offset_grad,
        gain_two_grad,
        shift_two_grad,
        up_weight_grad,
        up_offset_grad,
        down_weight_grad,
        down_offset_grad,
    )
    owned = (
        lax.psum_scatter(local_grads[0], "shard", scatter_dimension=0, tiled=True),
        lax.psum_scatter(local_grads[1], "shard", scatter_dimension=0, tiled=True),
        lax.psum_scatter(local_grads[2], "shard", scatter_dimension=0, tiled=True),
        lax.psum_scatter(local_grads[3], "shard", scatter_dimension=2, tiled=True),
        lax.psum_scatter(local_grads[4], "shard", scatter_dimension=1, tiled=True),
        lax.psum_scatter(local_grads[5], "shard", scatter_dimension=0, tiled=True),
        lax.psum_scatter(local_grads[6], "shard", scatter_dimension=0, tiled=True),
        lax.psum_scatter(local_grads[7], "shard", scatter_dimension=0, tiled=True),
        lax.psum_scatter(local_grads[8], "shard", scatter_dimension=0, tiled=True),
        lax.psum_scatter(local_grads[9], "shard", scatter_dimension=1, tiled=True),
        lax.psum_scatter(local_grads[10], "shard", scatter_dimension=1, tiled=True),
        lax.psum_scatter(local_grads[11], "shard", scatter_dimension=0, tiled=True),
    )
    totals = lax.psum(
        (
            owned[0],
            owned[1],
            owned[2],
            owned[3],
            owned[4],
            owned[5],
            owned[6],
            owned[7],
            owned[8],
            owned[9],
            owned[10],
            owned[11],
        ),
        "ctx",
    )
    block_out = block_out.reshape(row_count, row_tokens, model_width)
    in_grad = in_grad.reshape(row_count, row_tokens, model_width)
    block_out, in_grad = (
        lax.all_to_all(block_out, "ctx", split_axis=1, concat_axis=1, tiled=True),
        lax.all_to_all(in_grad, "ctx", split_axis=1, concat_axis=1, tiled=True),
    )
    return (block_out, in_grad) + tuple(totals)


MESH = pl.DeviceIdType.MESH
F32 = jnp.float32
BF16 = jnp.bfloat16
GAIN_ONE, SHIFT_ONE, PROJ_BIAS, GAIN_TWO, SHIFT_TWO, DOWN_BIAS, Q_BIAS, V_BIAS, UP_BIAS = range(9)
VEC_ROWS = 16
COPIES = 64
VMEM_LIMIT = 56 * 1024 * 1024


def mm(left, right, dims=((1,), (0,))):
    return lax.dot_general(left, right, (dims, ((), ())), preferred_element_type=F32)


NT = ((1,), (1,))
TN = ((0,), (0,))


def identity(size):
    at_row = lax.broadcasted_iota(jnp.int32, (size, size), 0)
    at_column = lax.broadcasted_iota(jnp.int32, (size, size), 1)
    return jnp.where(at_row == at_column, 1.0, 0.0).astype(BF16)


def pack_vectors(vec_ref, wide_ref, qv_ref, up_b_ref, shard):
    width = vec_ref.shape[1]
    depth = width // 4
    heads, _, piece = qv_ref.shape
    up_rows, up_piece = up_b_ref.shape
    vec_ref[...] = jnp.zeros_like(vec_ref)
    vec_ref[0:8, :depth] = wide_ref[...]
    wide = vec_ref[0:8, :]
    wide = pltpu.roll(wide, shard * depth, 1)
    span = 128 * ((4 * heads * piece + 127) // 128)
    qv_sum = jnp.zeros((8, span), F32)
    for head in range(heads):
        vec_ref[8:16, :] = jnp.zeros((8, width), F32)
        vec_ref[8:10, :piece] = qv_ref[head].astype(F32)
        qv_sum = qv_sum + pltpu.roll(vec_ref[8:16, :span], head * 4 * piece + shard * piece, 1)
    vec_ref[8:16, :] = jnp.zeros((8, width), F32)
    vec_ref[8 : 8 + up_rows, :up_piece] = up_b_ref[...].astype(F32)
    up_part = pltpu.roll(vec_ref[8:16, :128], shard * up_piece, 1)
    vec_ref[0:8, :] = wide
    vec_ref[Q_BIAS : Q_BIAS + 2, :span] = qv_sum[0:2]
    vec_ref[8:16, :128] = up_part


def finish_kernel(
    sums_ref, attn_pair, mlp_pair,
    out_ref, in_grad_ref, qkv_g_ref, proj_g_ref, up_g_ref, down_g_ref,
    gain_one_ref, shift_one_ref, proj_b_ref, gain_two_ref, shift_two_ref, down_b_ref, qv_g_ref, up_b_ref,
):
    attn_s3, attn_r3, mlp_s3, mlp_r3 = attn_pair.at[0], attn_pair.at[1], mlp_pair.at[0], mlp_pair.at[1]
    shard = lax.axis_index("shard")
    tokens, width = out_ref.shape
    vec_ref = sums_ref.at[2 * tokens : 2 * tokens + VEC_ROWS]
    depth = width // 4
    heads, _, piece = qv_g_ref.shape
    up_rows, up_piece = up_b_ref.shape
    out_ref[...] = sums_ref[0:tokens]
    in_grad_ref[...] = sums_ref[tokens : 2 * tokens]
    qkv_g_ref[...] = attn_s3[0:3].astype(F32) + attn_r3[0:3].astype(F32)
    unit = identity(depth)
    proj_g_ref[...] = mm(attn_s3[3], unit, TN) + mm(attn_r3[3], unit, TN)
    up_g_ref[...] = mlp_s3[0].astype(F32) + mlp_r3[0].astype(F32)
    down_g_ref[...] = mlp_s3[1].astype(F32) + mlp_r3[1].astype(F32)
    wide = pltpu.roll(vec_ref[0:8, :], lax.rem(width - shard * depth, width), 1)
    wide_refs = (gain_one_ref, shift_one_ref, proj_b_ref, gain_two_ref, shift_two_ref, down_b_ref)
    for index, ref in enumerate(wide_refs):
        ref[...] = wide[index : index + 1, :depth]
    span = 128 * ((4 * heads * piece + 127) // 128)
    for head in range(heads):
        turned = pltpu.roll(
            vec_ref[0:8, :span], lax.rem(span - head * 4 * piece - shard * piece, span), 1
        )
        qv_g_ref[head] = turned[Q_BIAS : Q_BIAS + 2, :piece]
    turned = pltpu.roll(vec_ref[8:16, :128], lax.rem(128 - shard * up_piece, 128), 1)
    up_b_ref[...] = turned[:up_rows, :up_piece]


def block_kernel(
    x_ref, cot_ref, seg_ref, qkv_w, proj_w, up_w, down_w, wide_ref, qv_ref, up_b_ref,
    sums_ref, attn_pair, mlp_pair,
    qkv_f, proj_t, proj_f, up_f, down_f, vec_ref, vec_in, segk, segk_in, x_in, dkv, dkv_in,
    part, ar_send, ar_recv, ar_all,
    attn_g, up_g, down_g, attn_s1, attn_r1, attn_s2, attn_r2,
    mlp_s1, mlp_r1, mlp_s2, mlp_r2,
    vec_s, vec_r, send_sem, recv_sem,
):
    attn_s3, attn_r3, mlp_s3, mlp_r3 = attn_pair.at[0], attn_pair.at[1], mlp_pair.at[0], mlp_pair.at[1]
    shard = lax.axis_index("shard")
    ctx = lax.axis_index("ctx")
    tp = lax.axis_index("tp")
    core = lax.rem(shard, 2)
    high = shard // 2
    s1 = shard + 1 - 2 * core
    s2 = lax.rem(shard + 2, 4)
    s3 = lax.rem(s1 + 2, 4)
    p1, p2, p3 = {"shard": s1}, {"shard": s2}, {"shard": s3}
    pc = {"ctx": 1 - ctx}
    tps = [lax.rem(tp + step, 4) for step in (1, 2, 3)]
    tokens, width = x_ref.shape
    depth = up_w.shape[0]
    heads_width = qkv_w.shape[2]
    head_count = heads_width // 64

    barrier = pltpu.get_barrier_semaphore()
    cross = [{"shard": index, "ctx": 1 - ctx} for index in (s1, s2, s3)]
    peers = [p1, p2, p3, pc] + cross + [{"tp": t} for t in tps]
    for peer in peers:
        pl.semaphore_signal(barrier, inc=1, device_id=peer, device_id_type=MESH)

    started = []

    def send(src, dst, peer):
        slot = len(started)
        copy = pltpu.make_async_remote_copy(
            src_ref=src, dst_ref=dst, send_sem=send_sem.at[slot], recv_sem=recv_sem.at[slot],
            device_id=peer, device_id_type=MESH,
        )
        copy.start()
        started.append(copy)
        return copy

    def unit_of(values):
        center = jnp.mean(values, axis=-1, keepdims=True)
        shifted = values - center
        inverse = lax.rsqrt(jnp.mean(shifted * shifted, axis=-1, keepdims=True) + EPSILON)
        return shifted * inverse, inverse

    pack_vectors(vec_ref, wide_ref, qv_ref, up_b_ref, shard)
    segk[...] = jnp.broadcast_to(seg_ref[...], segk.shape)
    proj_t[...] = mm(proj_w[...], identity(heads_width), TN).astype(BF16)
    pl.semaphore_wait(barrier, len(peers))

    def gather_start(local, full):
        far = send(local, full.at[shard], p2)
        near = send(local, full.at[shard], p1)
        return far, near

    def gather_pass(full, far):
        far.wait_recv()
        return send(full.at[s2], full.at[s2], p1)

    qkv_far, qkv_near = gather_start(qkv_w, qkv_f)
    vec_copies = [send(vec_ref, vec_in.at[i], p) for i, p in enumerate((p1, p2, p3))]
    x_copy = send(x_ref, x_in, pc)
    seg_copy = send(segk, segk_in, pc)
    qkv_f[shard] = qkv_w[...]
    proj_f[shard] = proj_t[...]
    up_f[shard] = up_w[...]
    down_f[shard] = down_w[...]
    residual_in = x_ref[...].astype(F32)
    unit_one, inverse_one = unit_of(residual_in)
    for copy in vec_copies:
        copy.wait_recv()
    vec = vec_ref[...] + vec_in[0] + vec_in[1] + vec_in[2]

    up_bias = jnp.concatenate(
        [vec[UP_BIAS + r : UP_BIAS + r + 1, :128] for r in range(up_b_ref.shape[0])], axis=1
    )

    def row(index, size=width):
        return vec[index : index + 1, :size]

    normed_one = (unit_one * row(GAIN_ONE) + row(SHIFT_ONE)).astype(BF16)
    x_copy.wait_recv()
    unit_other, _ = unit_of(x_in[...].astype(F32))
    normed_other = (unit_other * row(GAIN_ONE) + row(SHIFT_ONE)).astype(BF16)
    qkv_pass = gather_pass(qkv_f, qkv_far)
    proj_far, proj_near = gather_start(proj_t, proj_f)
    up_far, up_near = gather_start(up_w, up_f)
    down_far, down_near = gather_start(down_w, down_f)
    qkv_near.wait_recv()
    qkv_pass.wait_recv()
    weight_q, weight_k, weight_v = (
        qkv_f[:, index].reshape(4 * depth, heads_width) for index in range(3)
    )
    keys = mm(normed_one, weight_k).astype(BF16)
    values = (mm(normed_one, weight_v) + row(V_BIAS, heads_width)).astype(BF16)
    keys_other = mm(normed_other, weight_k).astype(BF16)
    values_other = (mm(normed_other, weight_v) + row(V_BIAS, heads_width)).astype(BF16)
    queries = (mm(normed_one, weight_q) + row(Q_BIAS, heads_width)).astype(BF16)

    lane_head = lax.broadcasted_iota(jnp.int32, (tokens, heads_width), 1) // 64
    of_head = [lane_head == index for index in range(head_count)]

    def pick(values_in, index):
        return jnp.where(of_head[index], values_in, jnp.zeros_like(values_in))

    seg_copy.wait_recv()
    query_at = lax.broadcasted_iota(jnp.int32, (tokens, tokens), 0)
    key_at = lax.broadcasted_iota(jnp.int32, (tokens, tokens), 1)
    segq = jnp.transpose(jnp.broadcast_to(seg_ref[...].astype(F32), (tokens, tokens))).astype(jnp.int32)
    allow_own = (key_at <= query_at) & (segq == segk[0:1, :])
    allow_other = (segq == segk_in[0:1, :]) & (key_at + tokens * (1 - ctx) <= query_at + tokens * ctx)
    query_of = [pick(queries, index) for index in range(head_count)]
    score_own = [
        jnp.where(allow_own, mm(query_of[i], keys, NT) * SCORE_SCALE, NEGATIVE)
        for i in range(head_count)
    ]
    proj_pass = gather_pass(proj_f, proj_far)
    probs_own, probs_other = [], []
    mixed_sum = jnp.zeros((tokens, heads_width), F32)
    for i in range(head_count):
        own = score_own[i]
        other = jnp.where(allow_other, mm(query_of[i], keys_other, NT) * SCORE_SCALE, NEGATIVE)
        top = jnp.maximum(
            jnp.max(own, axis=-1, keepdims=True), jnp.max(other, axis=-1, keepdims=True)
        )
        total = jnp.sum(jnp.exp(own - top), axis=-1, keepdims=True) + jnp.sum(
            jnp.exp(other - top), axis=-1, keepdims=True
        )
        log_total = top + jnp.log(total)
        probs_own.append(jnp.where(allow_own, jnp.exp(own - log_total), 0.0))
        probs_other.append(jnp.where(allow_other, jnp.exp(other - log_total), 0.0))
        mixed_head = mm(probs_own[i].astype(BF16), values) + mm(
            probs_other[i].astype(BF16), values_other
        )
        mixed_sum = mixed_sum + pick(mixed_head, i)
    mixed = mixed_sum.astype(BF16)

    def sum_start(phase, value):
        pieces = value.reshape(4, tokens // 4, width)
        part[phase] = pieces
        ar_send[phase] = pieces.astype(BF16)
        return [send(ar_send.at[phase, t], ar_recv.at[phase, i], {"tp": t}) for i, t in enumerate(tps)]

    def sum_pass(phase, copies):
        total = part[phase, tp]
        for i, copy in enumerate(copies):
            copy.wait_recv()
            total = total + ar_recv[phase, i].astype(F32)
        ar_all[phase, tp] = total.astype(BF16)
        return [send(ar_all.at[phase, tp], ar_all.at[phase, tp], {"tp": t}) for t in tps]

    def sum_end(phase, copies):
        for copy in copies:
            copy.wait_recv()
        return ar_all[phase].reshape(tokens, width).astype(F32)

    proj_near.wait_recv()
    proj_pass.wait_recv()
    weight_p = proj_f[...].reshape(4 * depth, heads_width)
    mid_sum = sum_start(0, mm(mixed, weight_p, NT))
    up_pass = gather_pass(up_f, up_far)
    mid_sum = sum_pass(0, mid_sum)
    down_pass = gather_pass(down_f, down_far)
    residual_mid = residual_in + sum_end(0, mid_sum) + row(PROJ_BIAS)
    unit_two, inverse_two = unit_of(residual_mid)
    normed_two = (unit_two * row(GAIN_TWO) + row(SHIFT_TWO)).astype(BF16)
    up_near.wait_recv()
    up_pass.wait_recv()
    up_full = up_f[...].reshape(4 * depth, up_f.shape[2])
    pre_gelu = mm(normed_two, up_full) + up_bias
    tangent = jnp.tanh(GELU_ROOT * (pre_gelu + GELU_CUBIC * pre_gelu * pre_gelu * pre_gelu))
    hidden = (0.5 * pre_gelu * (1.0 + tangent)).astype(BF16)
    slope = 0.5 * (1.0 + tangent) + 0.5 * pre_gelu * (1.0 - tangent * tangent) * GELU_ROOT * (
        1.0 + 3.0 * GELU_CUBIC * pre_gelu * pre_gelu
    )
    down_near.wait_recv()
    down_pass.wait_recv()
    down_full = down_f[...].reshape(4 * depth, down_f.shape[2])
    cot_low = cot_ref[...]
    cot_high = cot_low.astype(F32)
    pre_grad = mm(cot_low, down_full) * slope
    pre_grad_low = pre_grad.astype(BF16)
    two_sum = sum_start(2, mm(pre_grad_low, up_full, NT))
    out_sum = sum_start(1, mm(hidden, down_full, NT))

    def column_sum(value):
        return jnp.sum(value, axis=0, keepdims=True)

    vec_s[0] = jnp.zeros((VEC_ROWS, width), F32)
    up_bias_grad = column_sum(pre_grad)
    for r in range(up_b_ref.shape[0]):
        vec_s[0, UP_BIAS + r : UP_BIAS + r + 1, :128] = up_bias_grad[:, 128 * r : 128 * (r + 1)]
    vec_s[0, DOWN_BIAS : DOWN_BIAS + 1, :] = column_sum(cot_high)

    def reduce_one(grads, s1_buf, r1_buf):
        for half in range(2):
            s1_buf[half] = grads[2 * half + 1 - core].astype(BF16)
        return send(s1_buf, r1_buf, p1)

    def reduce_two(copy, grads, r1_buf, s2_buf, r2_buf):
        copy.wait_recv()
        s2_buf[...] = (grads[s2] + r1_buf[1 - high].astype(F32)).astype(BF16)
        return send(s2_buf, r2_buf, p2)

    def reduce_three(copy, grads, r1_buf, r2_buf, s3_buf, r3_buf):
        copy.wait_recv()
        s3_buf[...] = (
            grads[shard] + r1_buf[high].astype(F32) + r2_buf[...].astype(F32)
        ).astype(BF16)
        return send(s3_buf, r3_buf, pc)

    down_g[...] = mm(cot_low, hidden, TN).reshape(down_g.shape)
    down_copy = reduce_one(down_g, mlp_s1.at[1], mlp_r1.at[1])
    two_sum = sum_pass(2, two_sum)
    up_g[...] = mm(normed_two, pre_grad_low, TN).reshape(up_g.shape)
    up_copy = reduce_one(up_g, mlp_s1.at[0], mlp_r1.at[0])
    down_copy = reduce_two(down_copy, down_g, mlp_r1.at[1], mlp_s2.at[1], mlp_r2.at[1])
    norm_two_grad = sum_end(2, two_sum)
    vec_s[0, GAIN_TWO : GAIN_TWO + 1, :] = column_sum(norm_two_grad * unit_two)
    vec_s[0, SHIFT_TWO : SHIFT_TWO + 1, :] = column_sum(norm_two_grad)
    mid_grad = cot_high + normalize_back(norm_two_grad, unit_two, inverse_two, row(GAIN_TWO))
    vec_s[0, PROJ_BIAS : PROJ_BIAS + 1, :] = column_sum(mid_grad)
    mid_grad_low = mid_grad.astype(BF16)
    mixed_grad = mm(mid_grad_low, weight_p).astype(BF16)
    up_copy = reduce_two(up_copy, up_g, mlp_r1.at[0], mlp_s2.at[0], mlp_r2.at[0])
    delta_terms = mixed_grad.astype(F32) * mixed.astype(F32)
    zero = jnp.zeros((tokens, heads_width), F32)
    query_grad, key_own, value_own, key_other, value_other = zero, zero, zero, zero, zero
    for i in range(head_count):
        head_grad = pick(mixed_grad, i)
        delta = jnp.sum(pick(delta_terms, i), axis=-1, keepdims=True)
        grad_other = (probs_other[i] * (mm(head_grad, values_other, NT) - delta)).astype(BF16)
        grad_own = (probs_own[i] * (mm(head_grad, values, NT) - delta)).astype(BF16)
        key_other = key_other + mm(grad_other, query_of[i], TN)
        value_other = value_other + mm(probs_other[i].astype(BF16), head_grad, TN)
        key_own = key_own + mm(grad_own, query_of[i], TN)
        value_own = value_own + mm(probs_own[i].astype(BF16), head_grad, TN)
        query_grad = query_grad + pick(mm(grad_own, keys) + mm(grad_other, keys_other), i)
    dkv[0] = key_other.astype(BF16)
    dkv[1] = value_other.astype(BF16)
    dkv_copy = send(dkv, dkv_in, pc)
    down_copy = reduce_three(
        down_copy, down_g, mlp_r1.at[1], mlp_r2.at[1], mlp_s3.at[1], mlp_r3.at[1]
    )
    out_sum = sum_pass(1, out_sum)
    proj_grad = mm(mid_grad_low, mixed, TN).reshape(4, depth, heads_width)
    for index in range(4):
        attn_g[index, 3] = proj_grad[index]
    query_grad = query_grad * SCORE_SCALE
    query_low = query_grad.astype(BF16)
    vec_s[0, Q_BIAS : Q_BIAS + 1, :heads_width] = column_sum(query_grad)
    one_part = mm(query_low, weight_q, NT)
    dkv_copy.wait_recv()
    key_low = ((key_own + dkv_in[0].astype(F32)) * SCORE_SCALE).astype(BF16)
    value_grad = value_own + dkv_in[1].astype(F32)
    value_low = value_grad.astype(BF16)
    vec_s[0, V_BIAS : V_BIAS + 1, :heads_width] = column_sum(value_grad)
    one_part = one_part + mm(key_low, weight_k, NT) + mm(value_low, weight_v, NT)
    one_sum = sum_start(3, one_part)
    for index, grad_low in enumerate((query_low, key_low, value_low)):
        weight_grad = mm(normed_one, grad_low, TN).reshape(4, depth, heads_width)
        for block in range(4):
            attn_g[block, index] = weight_grad[block]
    attn_copy = reduce_one(attn_g, attn_s1, attn_r1)
    up_copy = reduce_three(up_copy, up_g, mlp_r1.at[0], mlp_r2.at[0], mlp_s3.at[0], mlp_r3.at[0])
    one_sum = sum_pass(3, one_sum)
    attn_copy = reduce_two(attn_copy, attn_g, attn_r1, attn_s2, attn_r2)
    norm_one_grad = sum_end(3, one_sum)
    vec_s[0, GAIN_ONE : GAIN_ONE + 1, :] = column_sum(norm_one_grad * unit_one)
    vec_s[0, SHIFT_ONE : SHIFT_ONE + 1, :] = column_sum(norm_one_grad)
    place = ctx * 4 + shard
    vec_copies = [send(vec_s.at[0], vec_r.at[place], p) for p in [p1, p2, p3, pc] + cross]
    vec_r[place] = vec_s[0]
    attn_copy = reduce_three(attn_copy, attn_g, attn_r1, attn_r2, attn_s3, attn_r3)
    sums_ref[tokens : 2 * tokens] = mid_grad + normalize_back(
        norm_one_grad, unit_one, inverse_one, row(GAIN_ONE)
    )
    sums_ref[0:tokens] = residual_mid + sum_end(1, out_sum) + row(DOWN_BIAS)
    for copy in vec_copies:
        copy.wait_recv()
    vec_total = vec_r[0]
    for index in range(1, 8):
        vec_total = vec_total + vec_r[index]
    sums_ref[2 * tokens : 2 * tokens + VEC_ROWS] = vec_total
    down_copy.wait_recv()
    up_copy.wait_recv()
    attn_copy.wait_recv()
    for copy in started:
        copy.wait_send()


def paired_body(
    block_in, segment_ids, out_cotangent, attn_gain, attn_shift, qkv_weight, qv_bias, proj_weight,
    proj_bias, mlp_gain, mlp_shift, up_weight, up_bias, down_weight, down_bias,
):
    _, tokens, width = block_in.shape
    depth = qkv_weight.shape[0]
    heads_width = qkv_weight.shape[2]
    units = up_weight.shape[1]
    head_count, head_piece = qv_bias.shape[1:]
    at_row = lax.broadcasted_iota(jnp.int32, (8, depth), 0)
    wide = jnp.zeros((8, depth), F32)
    vectors = (attn_gain, attn_shift, proj_bias, mlp_gain, mlp_shift, down_bias)
    for index, vector in enumerate(vectors):
        wide = jnp.where(at_row == index, vector.astype(F32)[None, :], wide)
    attn_shape = (4, depth, heads_width)
    mlp_shape = (depth, units)
    vmem = pltpu.VMEM
    shaped = jax.ShapeDtypeStruct
    middle_shapes = (
        shaped((2 * tokens + VEC_ROWS, width), F32),
        shaped((2,) + attn_shape, BF16),
        shaped((2, 2) + mlp_shape, BF16),
    )
    proj_shape = (depth, heads_width)
    qkv_shape = (3, depth, heads_width)
    scratch = [
        vmem((4,) + qkv_shape, BF16), vmem(proj_shape, BF16), vmem((4,) + proj_shape, BF16),
        vmem((4,) + mlp_shape, BF16), vmem((4,) + mlp_shape, BF16),
        vmem((VEC_ROWS, width), F32), vmem((3, VEC_ROWS, width), F32),
        vmem((8, tokens), jnp.int32), vmem((8, tokens), jnp.int32),
        vmem((tokens, width), BF16),
        vmem((2, tokens, heads_width), BF16), vmem((2, tokens, heads_width), BF16),
        vmem((4, 4, tokens // 4, width), F32), vmem((4, 4, tokens // 4, width), BF16),
        vmem((4, 3, tokens // 4, width), BF16), vmem((4, 4, tokens // 4, width), BF16),
        vmem((4,) + attn_shape, F32), vmem((4,) + mlp_shape, F32), vmem((4,) + mlp_shape, F32),
        vmem((2,) + attn_shape, BF16), vmem((2,) + attn_shape, BF16),
        vmem(attn_shape, BF16), vmem(attn_shape, BF16),
        vmem((2, 2) + mlp_shape, BF16), vmem((2, 2) + mlp_shape, BF16),
        vmem((2,) + mlp_shape, BF16), vmem((2,) + mlp_shape, BF16),
        vmem((1, VEC_ROWS, width), F32), vmem((8, VEC_ROWS, width), F32),
        pltpu.SemaphoreType.DMA((COPIES,)), pltpu.SemaphoreType.DMA((COPIES,)),
    ]
    whole = pl.BlockSpec(memory_space=pltpu.VMEM)
    middle = pl.pallas_call(
        block_kernel,
        out_shape=middle_shapes,
        in_specs=[whole] * 10,
        out_specs=(whole,) * 3,
        scratch_shapes=scratch,
        compiler_params=pltpu.CompilerParams(
            collective_id=0, has_side_effects=True, vmem_limit_bytes=VMEM_LIMIT
        ),
    )(
        block_in[0], out_cotangent[0], segment_ids, jnp.transpose(qkv_weight, (1, 0, 2)), proj_weight,
        up_weight, jnp.transpose(down_weight), wide, jnp.transpose(qv_bias, (1, 0, 2)), up_bias,
    )
    one_row = shaped((1, depth), F32)
    result_shapes = (
        shaped((tokens, width), F32), shaped((tokens, width), F32), shaped(qkv_shape, F32),
        shaped((heads_width, depth), F32), shaped(mlp_shape, F32), shaped(mlp_shape, F32),
        one_row, one_row, one_row, one_row, one_row, one_row,
        shaped((head_count, 2, head_piece), F32), shaped(up_bias.shape, F32),
    )
    (
        block_out, in_grad, qkv_g, proj_g, up_g, down_g,
        gain_one, shift_one, proj_b, gain_two, shift_two, down_b, qv_b, up_b,
    ) = pl.pallas_call(
        finish_kernel,
        out_shape=result_shapes,
        in_specs=[whole] * 3,
        out_specs=(whole,) * 14,
        compiler_params=pltpu.CompilerParams(vmem_limit_bytes=16 * 1024 * 1024),
    )(*middle)
    return (
        block_out[None], in_grad[None], gain_one[0], shift_one[0], jnp.transpose(qkv_g, (1, 0, 2)),
        jnp.transpose(qv_b, (1, 0, 2)), proj_g, proj_b[0], gain_two[0], shift_two[0], up_g, up_b,
        jnp.transpose(down_g), down_b[0],
    )


def solution(mesh):
    paired = mesh.shape["ctx"] == 2 and mesh.shape["shard"] == 4 and mesh.shape["tp"] == 4
    return jax.shard_map(
        paired_body if paired else body,
        mesh=mesh,
        in_specs=(
            P("shard", "ctx", None),
            P("shard", "ctx"),
            P("shard", "ctx", None),
            P("shard"),
            P("shard"),
            P("shard", None, "tp"),
            P(None, "tp", "shard"),
            P("tp", "shard"),
            P("shard"),
            P("shard"),
            P("shard"),
            P("shard", "tp"),
            P("tp", "shard"),
            P("tp", "shard"),
            P("shard"),
        ),
        out_specs=(
            P("shard", "ctx", None),
            P("shard", "ctx", None),
            P("shard"),
            P("shard"),
            P("shard", None, "tp"),
            P(None, "tp", "shard"),
            P("tp", "shard"),
            P("shard"),
            P("shard"),
            P("shard"),
            P("shard", "tp"),
            P("tp", "shard"),
            P("tp", "shard"),
            P("shard"),
        ),
        check_vma=False,
    )
```
